128 devices in a mesh: dp: 8 (over z, y_lo), tensor: 16 (over x, y_hi, core).
Axes of the slice: x: 4, y: 4 (y_hi: 2, y_lo: 2; y = y_hi * 2 + y_lo), z: 4, core: 2. Of those that a mesh axis runs over, the one named last changes fastest.
Arguments:
- activations: bfloat16 [256, 8192], P('dp'), may hold values from -6 to 6
- query_weight: bfloat16 [8192, 8192], P(None, 'tensor'), may hold values from -0.0625 to 0.0625
- output_weight: bfloat16 [8192, 8192], P('tensor'), may hold values from -0.375 to 0.375
- key_cache: bfloat16 [256, 8, 1024, 128], P(('dp', 'tensor'))
- value_cache: bfloat16 [256, 8, 1024, 128], P(('dp', 'tensor')), may hold values from -6 to 6
- fresh_pair: bfloat16 [256, 2, 1024], P(('dp', 'tensor')), may hold values from -6 to 6
- cache_length: int32 [256], P(('dp', 'tensor')), may hold values from 2 to 1024
- row_tenant: int32 [256], P('dp'), may hold values from 0 to 63, as said below
- tenant_slot: int32 [64], replicated, may hold values from 0 to 63, as said below
- query_deltas: bfloat16 [64, 128, 128, 128], P('dp', 'tensor'), may hold values from -0.1796875 to 0.1796875
- query_where: int32 [64, 128], P('dp', 'tensor'), may hold values from 0 to 255, as said below
- output_deltas: bfloat16 [64, 128, 128, 128], P('dp', 'tensor'), may hold values from -0.71875 to 0.71875
- output_where: int32 [64, 128], P('dp', 'tensor'), may hold values from 0 to 255, as said below
Outputs:
- layer_out: bfloat16 [256, 8192], P('dp', 'tensor')
The draws below stay inside these ranges and needn't reach their ends.
Inputs may be any that keep to these rules, and one draw needn't show every extreme that they name: A permutation: tenant t's tiles sit in slot tenant_slot[t], on dp index tenant_slot[t] // 8. `row_tenant`: among the requests of one dp group (32 consecutive rows), at most 8 have tenants stored on one dp index; one store receives exactly 8 from every group. `query_where`: within each block of 8 entries (one slot, one shard) the places are distinct. `output_where`: within each block of 8 entries (one slot, one shard) the places are distinct.
All inputs are finite; a program needn't handle non-finite values.
Results may differ from the reference program's by a relative error of at most 0.0089.
Values may be sent and summed in bfloat16 or wider, within the bound.
No kernel may reach another device: no remote copies, remote signals or barrier semaphores. Data moves between devices by JAX's collectives and lax.ppermute only.
A program may use at most 192 MiB of HBM per device.

```python
import jax
import jax.numpy as jnp
from jax import lax

D = 8192
H = 64
HD = 128
KVH = 8
TILE = 128
KS = 8
TEN_DEV = 8
CTX = 1024
COLS_DEV = 512
SHARD_TILES = 256
TILE_SLOTS = 128
GROUP_ROWS = 32
ROWS = 256
STORES = 8
TENANTS = 64
CAP = 8
N_TENSOR = 16


def tenant_layout(key):
    seeded = jax.random.fold_in(key, 4242)
    key_perm, key_busy, key_groups = jax.random.split(seeded, 3)
    slot_of = jax.random.permutation(key_perm, TENANTS).astype(jnp.int32)
    owner_of = jnp.argsort(slot_of).astype(jnp.int32)
    busy_store = jax.random.randint(key_busy, (), 0, STORES, dtype=jnp.int32)

    def one_group(group_key):
        key_pool, key_mix, key_local = jax.random.split(group_key, 3)
        others = (busy_store + 1 + jnp.arange(STORES - 1, dtype=jnp.int32)) % STORES
        pooled = jnp.repeat(others, CAP)
        pooled = jax.random.permutation(key_pool, pooled)[:GROUP_ROWS - CAP]
        chosen = jnp.concatenate([jnp.full((CAP,), busy_store, dtype=jnp.int32), pooled.astype(jnp.int32)])
        chosen = jax.random.permutation(key_mix, chosen)
        local_pick = jax.random.randint(key_local, (GROUP_ROWS,), 0, TEN_DEV, dtype=jnp.int32)
        return owner_of[chosen * TEN_DEV + local_pick]
    tenants = jax.vmap(one_group)(jax.random.split(key_groups, STORES))
    return (slot_of, tenants.reshape(ROWS).astype(jnp.int32))


def draw_tenant_slot(key, part):
    return tenant_layout(key)[0]


def draw_row_tenant(key, part):
    return tenant_layout(key)[1]


def tile_places(key, salt):
    all_keys = jax.random.split(jax.random.fold_in(key, salt), TENANTS * (TILE_SLOTS // KS))
    picks = jax.vmap(lambda one_key: jax.random.permutation(one_key, SHARD_TILES)[:KS])(all_keys)
    return picks.astype(jnp.int32).reshape(TENANTS, TILE_SLOTS)


def draw_query_where(key, part):
    return tile_places(key, 101)


def draw_output_where(key, part):
    return tile_places(key, 202)


def draw_key_cache(key, part):
    values = jax.random.normal(key, (ROWS, KVH, CTX, HD), jnp.float32)
    return values.astype(jnp.bfloat16)


def set_ends(values, key, least, top_value):
    dims = values.shape
    place = [jax.random.randint(jax.random.fold_in(key, axis), (), 0, dims[axis]) for axis in range(len(dims))]
    values = values.at[tuple(place)].set(least)
    longest = dims.index(max(dims))
    place[longest] = (place[longest] + 1) % dims[longest]
    return values.at[tuple(place)].set(top_value)


def level_of(rng, shape, cuts, low, high):
    level = 1.0
    for dim, shards_of in cuts:
        steps = jax.random.uniform(jax.random.fold_in(jax.random.fold_in(rng, 6), dim), (shards_of,), jnp.float32, low / len(cuts), high / len(cuts))
        level = level * jnp.repeat(jnp.exp(steps), shape[dim] // shards_of).reshape((-1,) + (1,) * (len(shape) - 1 - dim))
    return level


def noise(key, extent, scale, most, pieces=(), kind=jnp.bfloat16):
    factor_of = level_of(key, extent, pieces, -0.22, 0.18) if pieces else 1.0
    drawn = jax.random.normal(key, extent, jnp.float32) * scale * factor_of
    return jnp.minimum(jnp.maximum(drawn, -most), most).astype(kind)


def setup_inputs(seed: int = 0) -> dict:
    keys = jax.random.split(jax.random.key(seed), 14)
    return {
        "activations": noise(keys[0], (ROWS, D), 1.0, 6.0, ((0, 8),)),
        "query_weight": noise(keys[1], (D, H * HD), D ** -0.5, 0.0625, ((1, 16),)),
        "output_weight": noise(keys[2], (H * HD, D), (H * HD // 32) ** -0.5, 0.375, ((0, 16),)),
        "key_cache": draw_key_cache(jax.random.fold_in(keys[13], 71), 0),
        "value_cache": noise(keys[4], (ROWS, KVH, CTX, HD), 1.0, 6.0, ((0, 128),)),
        "fresh_pair": noise(keys[5], (ROWS, 2, KVH * HD), 1.0, 6.0, ((0, 128),)),
        "cache_length": set_ends(jax.random.randint(keys[6], (ROWS,), 2, CTX + 1), jax.random.fold_in(keys[6], 1), 2, CTX).astype(jnp.int32),
        "row_tenant": draw_row_tenant(jax.random.fold_in(keys[13], 71), 0),
        "tenant_slot": draw_tenant_slot(jax.random.fold_in(keys[13], 71), 0),
        "query_deltas": noise(keys[9], (TENANTS, TILE_SLOTS, TILE, TILE), 0.03, 0.1796875, ((0, 8), (1, 16))),
        "query_where": draw_query_where(jax.random.fold_in(keys[13], 71), 0),
        "output_deltas": noise(keys[11], (TENANTS, TILE_SLOTS, TILE, TILE), 0.12, 0.71875, ((0, 8), (1, 16))),
        "output_where": draw_output_where(jax.random.fold_in(keys[13], 71), 0),
    }


def apply_tiles(inputs, row_slot, deltas, where_list, first_slot, out_columns):
    tile_size = deltas.shape[-1]
    slot_count = where_list.shape[0]
    per_slot = where_list.shape[1]
    out_tiles = out_columns // tile_size
    blocks = inputs.reshape(inputs.shape[0], inputs.shape[1] // tile_size, tile_size)
    flat_places = where_list.reshape(slot_count * per_slot)
    source = flat_places // out_tiles
    target = flat_places % out_tiles
    picked = jnp.take(blocks, source, axis=1)
    owners = first_slot + jnp.arange(slot_count * per_slot, dtype=jnp.int32) // per_slot
    chosen = row_slot[:, None] == owners[None, :]
    picked = jnp.where(chosen[:, :, None], picked, jnp.zeros((), inputs.dtype))
    products = jnp.einsum("rkt,kts->rks", picked.astype(jnp.float32), deltas.reshape(slot_count * per_slot, tile_size, tile_size).astype(jnp.float32))
    spread = (target[:, None] == jnp.arange(out_tiles, dtype=jnp.int32)[None, :]).astype(jnp.float32)
    combined = jnp.einsum("rks,kb->rbs", products, spread, precision=lax.Precision.HIGHEST)
    return combined.reshape(inputs.shape[0], out_columns)


def attend(query_rows, key_cache, value_cache, fresh_pair, cache_length):
    count_rows, kv_heads, context, head_dim = key_cache.shape
    grouped = query_rows.reshape(count_rows, kv_heads, -1, head_dim).astype(jnp.float32)
    score_scale = head_dim ** -0.5
    scores = jnp.einsum("rkgd,rkld->rkgl", grouped, key_cache.astype(jnp.float32)) * score_scale
    fresh_key = fresh_pair[:, 0].reshape(count_rows, kv_heads, head_dim).astype(jnp.float32)
    fresh_value = fresh_pair[:, 1].reshape(count_rows, kv_heads, head_dim).astype(jnp.float32)
    own_score = jnp.einsum("rkgd,rkd->rkg", grouped, fresh_key) * score_scale
    position = jnp.arange(context, dtype=jnp.int32)
    visible = (position[None, :] < cache_length[:, None])[:, None, None, :]
    scores = jnp.where(visible, scores, -1e30)
    highest = jnp.maximum(jnp.max(scores, axis=3), own_score)
    weights = jnp.where(visible, jnp.exp(scores - highest[..., None]), 0.0)
    own_weight = jnp.exp(own_score - highest)
    denominator = jnp.sum(weights, axis=3) + own_weight
    probabilities = (weights / denominator[..., None]).astype(jnp.bfloat16)
    own_probability = (own_weight / denominator).astype(jnp.bfloat16)
    mixed = jnp.einsum("rkgl,rkld->rkgd", probabilities.astype(jnp.float32), value_cache.astype(jnp.float32))
    mixed = mixed + own_probability.astype(jnp.float32)[..., None] * fresh_value[:, :, None, :]
    return mixed.astype(jnp.bfloat16).reshape(count_rows, -1)


def reference(activations, query_weight, output_weight, key_cache, value_cache, fresh_pair, cache_length, row_tenant, tenant_slot, query_deltas, query_where, output_deltas, output_where):
    row_slot = jnp.take(tenant_slot, row_tenant)
    query_parts = []
    for shard_index in range(N_TENSOR):
        query_parts.append(apply_tiles(activations, row_slot, query_deltas[:, shard_index * KS:(shard_index + 1) * KS], query_where[:, shard_index * KS:(shard_index + 1) * KS], 0, COLS_DEV))
    query_extra = jnp.concatenate(query_parts, axis=1)
    query_heads = (jnp.dot(activations, query_weight, preferred_element_type=jnp.float32) + query_extra).astype(jnp.bfloat16)
    attended = attend(query_heads, key_cache, value_cache, fresh_pair, cache_length)
    out_extra = jnp.zeros((activations.shape[0], D), jnp.float32)
    for shard_index in range(N_TENSOR):
        heads_part = attended[:, shard_index * COLS_DEV:(shard_index + 1) * COLS_DEV]
        out_extra = out_extra + apply_tiles(heads_part, row_slot, output_deltas[:, shard_index * KS:(shard_index + 1) * KS], output_where[:, shard_index * KS:(shard_index + 1) * KS], 0, D)
    layer_out = jnp.dot(attended, output_weight, preferred_element_type=jnp.float32) + out_extra
    return layer_out.astype(jnp.bfloat16)
```

```python
import functools

import jax
import jax.numpy as jnp
from jax import lax
from jax.experimental import pallas as pl
from jax.experimental.pallas import tpu as pltpu
from jax.sharding import PartitionSpec as P

F32 = jnp.float32
BF16 = jnp.bfloat16
I32 = jnp.int32
LANES = 128
EVERY = ("dp", "tensor")


def iota(shape, axis):
    return lax.broadcasted_iota(I32, shape, axis)


def dot(a, b, contract=((1,), (0,))):
    return lax.dot_general(a, b, (contract, ((), ())), preferred_element_type=F32)


def pick(mask, value=1.0):
    return jnp.where(mask, value, 0.0)


def pack_kernel(per_store, tenant_ref, slot_ref, rows_ref, out_ref, place_ref):
    group = lax.axis_index("dp")
    count, width = rows_ref.shape
    tenants = slot_ref.shape[1]
    places = out_ref.shape[0]
    capacity = 8
    stores = places // capacity
    chosen = pick(iota((tenants, count), 0) == tenant_ref[...]).astype(BF16)
    table = jnp.broadcast_to(slot_ref[...].astype(F32), (8, tenants)).astype(BF16)
    slot = dot(table, chosen)[0:1].astype(I32)
    store = slot // per_store
    at_store = pick(iota((stores, count), 0) == store)
    earlier = pick(iota((count, count), 0) < iota((count, count), 1)).astype(BF16)
    before = dot(at_store.astype(BF16), earlier)
    rank = jnp.sum(at_store * before, axis=0, keepdims=True).astype(I32)
    placed = iota((places, count), 0) == store * capacity + rank
    one_hot = pick(placed)
    place_ref[...] = one_hot.astype(BF16)
    hot = one_hot.astype(BF16)
    step = 1024
    for start in range(0, width, step):
        block = dot(hot, rows_ref[:, start : start + step])
        out_ref[:, start : start + step] = block.astype(BF16)
    number = iota((1, count), 1) + 1
    lane_of = iota((LANES, count), 0) % (LANES // 2)
    spread = jnp.where(lane_of == group * capacity + rank, number, 0).astype(F32).astype(BF16)
    by_lane = dot(at_store.astype(BF16), spread, ((1,), (1,)))
    wide = jnp.broadcast_to(by_lane[:, None, :], (stores, capacity, LANES))
    out_ref[:, width : width + LANES] = wide.reshape(places, LANES).astype(BF16)
    slot_col = jnp.sum(jnp.where(placed, slot + 1, 0).astype(F32), axis=1, keepdims=True)
    row_col = jnp.sum(jnp.where(placed, number, 0).astype(F32), axis=1, keepdims=True)
    lane = iota((places, LANES), 1)
    facts = jnp.where(lane == 0, slot_col, jnp.where(lane == 1, row_col, 0.0))
    out_ref[:, width + LANES : width + 2 * LANES] = facts.astype(BF16)


def pack_rows(row_tenant, tenant_slot, rows, places, per_store):
    count, width = rows.shape
    return pl.pallas_call(
        functools.partial(pack_kernel, per_store),
        out_shape=(
            jax.ShapeDtypeStruct((places, width + 2 * LANES), BF16),
            jax.ShapeDtypeStruct((places, count), BF16),
        ),
        compiler_params=pltpu.CompilerParams(vmem_limit_bytes=8 << 20),
        name="pack_rows",
    )(row_tenant.reshape(1, count), tenant_slot.reshape(1, -1), rows)


def query_kernel(where_ref, arrived_ref, tiles_ref, base_ref, out_ref, facts_ref, total):
    me = lax.axis_index("dp")
    slots, per_slot, tile = tiles_ref.shape[:3]
    places = arrived_ref.shape[0]
    width = arrived_ref.shape[1] - 2 * LANES
    blocks = total.shape[1] // tile
    group_rows = base_ref.shape[0] // blocks
    groups = out_ref.shape[0] // base_ref.shape[0]
    capacity = places // groups
    facts = arrived_ref[:, width + LANES : width + 2 * LANES].astype(F32)
    facts_ref[...] = facts
    own_slot = facts[:, 0:1].astype(I32) - 1 - me * slots
    total[...] = jnp.zeros_like(total)
    for t in range(slots):
        mine = own_slot == t
        for k in range(per_slot):
            place = where_ref[t, k]
            source = pl.multiple_of((place // blocks) * tile, tile)
            target = pl.multiple_of((place % blocks) * tile, tile)
            product = dot(arrived_ref[:, pl.ds(source, tile)], tiles_ref[t, k])
            total[:, pl.ds(target, tile)] += jnp.where(mine, product, 0.0)
    stacked = jnp.concatenate(
        [total[:, b * tile : (b + 1) * tile] for b in range(blocks)], axis=0
    ).astype(BF16)
    by_lane = arrived_ref[:, width : width + LANES].astype(F32)
    by_lane = jnp.sum(by_lane.reshape(groups, capacity, LANES), axis=0)[0:1].astype(I32)
    lane = iota((1, LANES), 1)
    home = (lane % places) // capacity * group_rows + by_lane - 1
    home = jnp.where(by_lane > 0, home * blocks + lane // places, -blocks)
    block_rows = group_rows * blocks
    for g in range(groups):
        row = iota((block_rows, LANES), 0) + g * block_rows
        expand = jnp.concatenate(
            [pick(row == home + b).astype(BF16) for b in range(0, blocks, LANES // places)],
            axis=1,
        )
        sent = dot(expand, stacked) + jnp.where(me == g, base_ref[...], 0.0)
        out_ref[g * block_rows : (g + 1) * block_rows, :] = sent.astype(BF16)


def query_visit(arrived, tiles, where, base, groups):
    places = arrived.shape[0]
    slots, per_slot, tile = tiles.shape[:3]
    columns = base.shape[1]
    blocks = columns // tile
    stacked = base.reshape(base.shape[0] * blocks, tile)
    vmem = pl.BlockSpec(memory_space=pltpu.VMEM)
    return pl.pallas_call(
        query_kernel,
        out_shape=(
            jax.ShapeDtypeStruct((groups * stacked.shape[0], tile), BF16),
            jax.ShapeDtypeStruct((places, LANES), F32),
        ),
        in_specs=[pl.BlockSpec(memory_space=pltpu.SMEM), vmem, vmem, vmem],
        scratch_shapes=[pltpu.VMEM((places, columns), F32)],
        compiler_params=pltpu.CompilerParams(vmem_limit_bytes=12 << 20),
        name="query_visit",
    )(where, arrived, tiles, stacked)


def attend_kernel(
    length_ref, arrived_ref, fresh_ref, key_ref, value_ref, out_ref, keys, values, key_sem, value_sem
):
    requests, kv_heads, context, size = key_ref.shape
    for i in range(requests):
        pltpu.make_async_copy(key_ref.at[i], keys.at[i], key_sem.at[i]).start()
    for i in range(requests):
        pltpu.make_async_copy(value_ref.at[i], values.at[i], value_sem.at[i]).start()
    shards = out_ref.shape[1]
    stores = arrived_ref.shape[0]
    scale = size ** (-0.5)
    query = arrived_ref[0].astype(F32)
    for s in range(1, stores):
        query = query + arrived_ref[s].astype(F32)
    fresh = fresh_ref[...].astype(F32)
    upper = iota((8, size), 0) < 4
    position = iota((1, context), 1)
    mixed = [[None] * kv_heads for _ in range(requests)]
    for i in range(requests):
        pltpu.make_async_copy(key_ref.at[i], keys.at[i], key_sem.at[i]).wait()
        visible = position < length_ref[i]
        parts = []
        for g in range(kv_heads):
            first, second = query[2 * g], query[2 * g + 1]
            if i == 0:
                heads = jnp.where(upper, first, pltpu.roll(second, 4, 0))
            else:
                heads = jnp.where(upper, pltpu.roll(first, 4, 0), second)
            heads = heads.astype(BF16)
            scores = dot(heads, keys[i, g], ((1,), (1,))) * scale
            fresh_key = fresh[i, 0:1, g * size : (g + 1) * size]
            own = jnp.sum(heads.astype(F32) * fresh_key, axis=1, keepdims=True) * scale
            scores = jnp.where(visible, scores, -1e30)
            highest = jnp.maximum(jnp.max(scores, axis=1, keepdims=True), own)
            weights = jnp.where(visible, jnp.exp(scores - highest), 0.0)
            own_weight = jnp.exp(own - highest)
            total = jnp.sum(weights, axis=1, keepdims=True) + own_weight
            share = (weights / total).astype(BF16)
            own_share = (own_weight / total).astype(BF16).astype(F32)
            parts.append((share, own_share))
        pltpu.make_async_copy(value_ref.at[i], values.at[i], value_sem.at[i]).wait()
        for g in range(kv_heads):
            share, own_share = parts[g]
            fresh_value = fresh[i, 1:2, g * size : (g + 1) * size]
            mixed[i][g] = dot(share, values[i, g]) + own_share * fresh_value
    for g in range(kv_heads):
        one, two = mixed[0][g], mixed[1][g]
        first = jnp.where(upper, one, pltpu.roll(two, 4, 0)).astype(BF16)
        second = jnp.where(upper, pltpu.roll(one, 4, 0), two).astype(BF16)
        for d in range(out_ref.shape[0]):
            out_ref[d, 2 * g] = first
            out_ref[d, 2 * g + 1] = second


def attend(arrived, keys, values, fresh, lengths, groups):
    requests, kv_heads, context, size = keys.shape
    shards = arrived.shape[0] // (groups * 8)
    vmem = pl.BlockSpec(memory_space=pltpu.VMEM)
    hbm = pl.BlockSpec(memory_space=pl.ANY)
    return pl.pallas_call(
        attend_kernel,
        out_shape=jax.ShapeDtypeStruct((groups, shards, 8, size), BF16),
        in_specs=[pl.BlockSpec(memory_space=pltpu.SMEM), vmem, vmem, hbm, hbm],
        scratch_shapes=[
            pltpu.VMEM(keys.shape, BF16),
            pltpu.VMEM(values.shape, BF16),
            pltpu.SemaphoreType.DMA((requests,)),
            pltpu.SemaphoreType.DMA((requests,)),
        ],
        compiler_params=pltpu.CompilerParams(vmem_limit_bytes=24 << 20),
        name="attend",
    )(lengths, arrived.reshape(groups, shards, 8, size), fresh, keys, values)


def output_kernel(
    where_ref, arrived_ref, facts_ref, tiles_ref, weight_ref, out_ref, weight, rows, total, sems
):
    me = lax.axis_index("dp")
    slots, per_slot, tile = tiles_ref.shape[:3]
    groups, shards, capacity, columns = out_ref.shape
    places = groups * capacity
    depth, width = weight_ref.shape
    chunks = sems.shape[0]
    chunk = width // chunks

    def fetch(c):
        span = pl.ds(c * chunk, chunk)
        return pltpu.make_async_copy(weight_ref.at[:, span], weight.at[:, span], sems.at[c])

    for c in range(chunks):
        fetch(c).start()
    blocks = depth // tile
    group_rows = arrived_ref.shape[0] // (groups * blocks)
    facts = facts_ref[...].astype(I32)
    own_slot = facts[:, 0:1] - 1 - me * slots
    number = facts[:, 1:2]
    home = iota((places, 1), 0) // capacity * group_rows + number - 1
    home = jnp.where(number > 0, home * blocks, -blocks)
    lane = iota((places, arrived_ref.shape[0]), 1)
    for b in range(blocks):
        gather = pick(lane == home + b).astype(BF16)
        rows[:, b * tile : (b + 1) * tile] = dot(gather, arrived_ref[...]).astype(BF16)
    total[...] = jnp.zeros_like(total)
    targets = width // tile
    for t in range(slots):
        mine = own_slot == t
        for k in range(per_slot):
            place = where_ref[t, k]
            source = pl.multiple_of((place // targets) * tile, tile)
            target = pl.multiple_of((place % targets) * tile, tile)
            product = dot(rows[:, pl.ds(source, tile)], tiles_ref[t, k])
            total[:, pl.ds(target, tile)] += jnp.where(mine, product, 0.0)
    per_chunk = chunk // columns
    for c in range(chunks):
        fetch(c).wait()
        for n in range(per_chunk):
            shard = c * per_chunk + n
            span = slice(shard * columns, (shard + 1) * columns)
            result = dot(rows[...], weight[:, span]) + total[:, span]
            out_ref[:, shard] = result.reshape(groups, capacity, columns).astype(BF16)


def output_visit(arrived, facts, tiles, where, weight, groups):
    depth, width = weight.shape
    places = facts.shape[0]
    shards = width // depth
    chunks = 8
    vmem = pl.BlockSpec(memory_space=pltpu.VMEM)
    return pl.pallas_call(
        output_kernel,
        out_shape=jax.ShapeDtypeStruct((groups, shards, places // groups, depth), BF16),
        in_specs=[
            pl.BlockSpec(memory_space=pltpu.SMEM),
            vmem,
            vmem,
            vmem,
            pl.BlockSpec(memory_space=pl.ANY),
        ],
        scratch_shapes=[
            pltpu.VMEM((depth, width), BF16),
            pltpu.VMEM((places, depth), BF16),
            pltpu.VMEM((places, width), F32),
            pltpu.SemaphoreType.DMA((chunks,)),
        ],
        compiler_params=pltpu.CompilerParams(vmem_limit_bytes=24 << 20),
        name="output_visit",
    )(where, arrived, facts, tiles, weight)


def finish_kernel(arrived_ref, place_ref, out_ref):
    stores, shards, capacity, columns = arrived_ref.shape
    total = arrived_ref[:, 0].astype(F32)
    for j in range(1, shards):
        total = total + arrived_ref[:, j].astype(F32)
    rounded = total.reshape(stores * capacity, columns).astype(BF16)
    out_ref[...] = dot(place_ref[...], rounded, ((0,), (0,))).astype(BF16)


def finish(arrived, place):
    return pl.pallas_call(
        finish_kernel,
        out_shape=jax.ShapeDtypeStruct((place.shape[1], arrived.shape[3]), BF16),
        compiler_params=pltpu.CompilerParams(vmem_limit_bytes=8 << 20),
        name="finish",
    )(arrived, place)


def swap(blocks, axes):
    return lax.all_to_all(blocks, axes, split_axis=0, concat_axis=0, tiled=True)


def body(
    activations,
    query_weight,
    output_weight,
    key_cache,
    value_cache,
    fresh_pair,
    cache_length,
    row_tenant,
    tenant_slot,
    query_deltas,
    query_where,
    output_deltas,
    output_where,
):
    groups = lax.axis_size("dp")
    shards = lax.axis_size("tensor")
    per_store = query_deltas.shape[0]
    capacity = 8
    packed, place = pack_rows(row_tenant, tenant_slot, activations, groups * capacity, per_store)
    arrived = swap(packed, "dp")
    base_query = jnp.dot(activations, query_weight, preferred_element_type=F32)
    sent_query, facts = query_visit(arrived, query_deltas, query_where, base_query, groups)
    query = swap(sent_query, EVERY)
    attended = attend(query, key_cache, value_cache, fresh_pair, cache_length, groups)
    size = attended.shape[3]
    rows = swap(attended.reshape(-1, size), EVERY)
    parts = output_visit(rows, facts, output_deltas, output_where, output_weight, groups)
    columns = parts.shape[3]
    summed = swap(parts.reshape(-1, columns), EVERY)
    return finish(summed.reshape(groups, shards, capacity, columns), place)


def solution(mesh):
    placed = (
        P("dp", None),
        P(None, "tensor"),
        P("tensor", None),
        P(("dp", "tensor"), None, None, None),
        P(("dp", "tensor"), None, None, None),
        P(("dp", "tensor"), None, None),
        P(("dp", "tensor")),
        P("dp"),
        P(),
        P("dp", "tensor", None, None),
        P("dp", "tensor"),
        P("dp", "tensor", None, None),
        P("dp", "tensor"),
    )
    return jax.shard_map(
        body, mesh=mesh, in_specs=placed, out_specs=P("dp", "tensor"), check_vma=False
    )
```

```python
import functools

import jax
import jax.numpy as jnp
from jax import lax
from jax.experimental import pallas as pl
from jax.experimental.pallas import tpu as pltpu
from jax.sharding import PartitionSpec as P

F32 = jnp.float32
BF16 = jnp.bfloat16
I32 = jnp.int32
LANES = 128
EVERY = ("dp", "tensor")
COST = pl.CostEstimate(flops=1 << 35, bytes_accessed=48 << 20, transcendentals=0)


def iota(shape, axis):
    return lax.broadcasted_iota(I32, shape, axis)


def dot(a, b, contract=((1,), (0,))):
    return lax.dot_general(a, b, (contract, ((), ())), preferred_element_type=F32)


def pick(mask, value=1.0):
    return jnp.where(mask, value, 0.0)


def pack_kernel(per_store, tenant_ref, slot_ref, rows_ref, out_ref, place_ref):
    group = lax.axis_index("dp")
    count, width = rows_ref.shape
    tenants = slot_ref.shape[1]
    places = out_ref.shape[0]
    capacity = 8
    stores = places // capacity
    chosen = pick(iota((tenants, count), 0) == tenant_ref[...]).astype(BF16)
    table = jnp.broadcast_to(slot_ref[...].astype(F32), (8, tenants)).astype(BF16)
    slot = dot(table, chosen)[0:1].astype(I32)
    store = slot // per_store
    at_store = pick(iota((stores, count), 0) == store)
    earlier = pick(iota((count, count), 0) < iota((count, count), 1)).astype(BF16)
    before = dot(at_store.astype(BF16), earlier)
    rank = jnp.sum(at_store * before, axis=0, keepdims=True).astype(I32)
    placed = iota((places, count), 0) == store * capacity + rank
    one_hot = pick(placed)
    place_ref[...] = one_hot.astype(BF16)
    hot = one_hot.astype(BF16)
    step = 1024
    for start in range(0, width, step):
        block = dot(hot, rows_ref[:, start : start + step])
        out_ref[:, start : start + step] = block.astype(BF16)
    number = iota((1, count), 1) + 1
    lane_of = iota((LANES, count), 0) % (LANES // 2)
    spread = jnp.where(lane_of == group * capacity + rank, number, 0).astype(F32).astype(BF16)
    by_lane = dot(at_store.astype(BF16), spread, ((1,), (1,)))
    wide = jnp.broadcast_to(by_lane[:, None, :], (stores, capacity, LANES))
    out_ref[:, width : width + LANES] = wide.reshape(places, LANES).astype(BF16)
    slot_col = jnp.sum(jnp.where(placed, slot + 1, 0).astype(F32), axis=1, keepdims=True)
    row_col = jnp.sum(jnp.where(placed, number, 0).astype(F32), axis=1, keepdims=True)
    lane = iota((places, LANES), 1)
    facts = jnp.where(lane == 0, slot_col, jnp.where(lane == 1, row_col, 0.0))
    out_ref[:, width + LANES : width + 2 * LANES] = facts.astype(BF16)


def pack_rows(row_tenant, tenant_slot, rows, places, per_store):
    count, width = rows.shape
    return pl.pallas_call(
        functools.partial(pack_kernel, per_store),
        out_shape=(
            jax.ShapeDtypeStruct((places, width + 2 * LANES), BF16),
            jax.ShapeDtypeStruct((places, count), BF16),
        ),
        compiler_params=pltpu.CompilerParams(vmem_limit_bytes=8 << 20),
        name="pack_rows",
    )(row_tenant.reshape(1, count), tenant_slot.reshape(1, -1), rows)


def query_kernel(where_ref, arrived_ref, tiles_ref, base_ref, out_ref, facts_ref, total):
    me = lax.axis_index("dp")
    slots, per_slot, tile = tiles_ref.shape[:3]
    places = arrived_ref.shape[0]
    width = arrived_ref.shape[1] - 2 * LANES
    blocks = total.shape[1] // tile
    group_rows = base_ref.shape[0] // blocks
    groups = out_ref.shape[0] // base_ref.shape[0]
    capacity = places // groups
    facts = arrived_ref[:, width + LANES : width + 2 * LANES].astype(F32)
    facts_ref[...] = facts
    own_slot = facts[:, 0:1].astype(I32) - 1 - me * slots
    total[...] = jnp.zeros_like(total)
    for t in range(slots):
        mine = own_slot == t
        for k in range(per_slot):
            place = where_ref[t, k]
            source = pl.multiple_of((place // blocks) * tile, tile)
            target = pl.multiple_of((place % blocks) * tile, tile)
            product = dot(arrived_ref[:, pl.ds(source, tile)], tiles_ref[t, k])
            total[:, pl.ds(target, tile)] += jnp.where(mine, product, 0.0)
    stacked = jnp.concatenate(
        [total[:, b * tile : (b + 1) * tile] for b in range(blocks)], axis=0
    ).astype(BF16)
    by_lane = arrived_ref[:, width : width + LANES].astype(F32)
    by_lane = jnp.sum(by_lane.reshape(groups, capacity, LANES), axis=0)[0:1].astype(I32)
    lane = iota((1, LANES), 1)
    home = (lane % places) // capacity * group_rows + by_lane - 1
    home = jnp.where(by_lane > 0, home * blocks + lane // places, -blocks)
    block_rows = group_rows * blocks
    for g in range(groups):
        row = iota((block_rows, LANES), 0) + g * block_rows
        expand = jnp.concatenate(
            [pick(row == home + b).astype(BF16) for b in range(0, blocks, LANES // places)],
            axis=1,
        )
        sent = dot(expand, stacked) + jnp.where(me == g, base_ref[...], 0.0)
        out_ref[g * block_rows : (g + 1) * block_rows, :] = sent.astype(BF16)


def query_visit(arrived, tiles, where, base, groups):
    places = arrived.shape[0]
    slots, per_slot, tile = tiles.shape[:3]
    columns = base.shape[1]
    blocks = columns // tile
    stacked = base.reshape(base.shape[0] * blocks, tile)
    vmem = pl.BlockSpec(memory_space=pltpu.VMEM)
    return pl.pallas_call(
        query_kernel,
        out_shape=(
            jax.ShapeDtypeStruct((groups * stacked.shape[0], tile), BF16),
            jax.ShapeDtypeStruct((places, LANES), F32),
        ),
        in_specs=[pl.BlockSpec(memory_space=pltpu.SMEM), vmem, vmem, vmem],
        scratch_shapes=[pltpu.VMEM((places, columns), F32)],
        cost_estimate=COST,
        compiler_params=pltpu.CompilerParams(vmem_limit_bytes=12 << 20),
        name="query_visit",
    )(where, arrived, tiles, stacked)


def attend_kernel(
    length_ref, arrived_ref, fresh_ref, keys, values, out_ref
):
    requests, kv_heads, context, size = keys.shape
    shards = out_ref.shape[1]
    stores = arrived_ref.shape[0]
    scale = size ** (-0.5)
    query = arrived_ref[0].astype(F32)
    for s in range(1, stores):
        query = query + arrived_ref[s].astype(F32)
    fresh = fresh_ref[...].astype(F32)
    upper = iota((8, size), 0) < 4
    position = iota((1, context), 1)
    mixed = [[None] * kv_heads for _ in range(requests)]
    for i in range(requests):
        visible = position < length_ref[i]
        parts = []
        for g in range(kv_heads):
            first, second = query[2 * g], query[2 * g + 1]
            if i == 0:
                heads = jnp.where(upper, first, pltpu.roll(second, 4, 0))
            else:
                heads = jnp.where(upper, pltpu.roll(first, 4, 0), second)
            heads = heads.astype(BF16)
            scores = dot(heads, keys[i, g], ((1,), (1,))) * scale
            fresh_key = fresh[i, 0:1, g * size : (g + 1) * size]
            own = jnp.sum(heads.astype(F32) * fresh_key, axis=1, keepdims=True) * scale
            scores = jnp.where(visible, scores, -1e30)
            highest = jnp.maximum(jnp.max(scores, axis=1, keepdims=True), own)
            weights = jnp.where(visible, jnp.exp(scores - highest), 0.0)
            own_weight = jnp.exp(own - highest)
            total = jnp.sum(weights, axis=1, keepdims=True) + own_weight
            share = (weights / total).astype(BF16)
            own_share = (own_weight / total).astype(BF16).astype(F32)
            parts.append((share, own_share))
        for g in range(kv_heads):
            share, own_share = parts[g]
            fresh_value = fresh[i, 1:2, g * size : (g + 1) * size]
            mixed[i][g] = dot(share, values[i, g]) + own_share * fresh_value
    for g in range(kv_heads):
        one, two = mixed[0][g], mixed[1][g]
        first = jnp.where(upper, one, pltpu.roll(two, 4, 0)).astype(BF16)
        second = jnp.where(upper, pltpu.roll(one, 4, 0), two).astype(BF16)
        for d in range(out_ref.shape[0]):
            out_ref[d, 2 * g] = first
            out_ref[d, 2 * g + 1] = second


def attend(arrived, keys, values, fresh, lengths, groups):
    requests, kv_heads, context, size = keys.shape
    shards = arrived.shape[0] // (groups * 8)
    vmem = pl.BlockSpec(memory_space=pltpu.VMEM)
    return pl.pallas_call(
        attend_kernel,
        out_shape=jax.ShapeDtypeStruct((groups, shards, 8, size), BF16),
        in_specs=[pl.BlockSpec(memory_space=pltpu.SMEM), vmem, vmem, vmem, vmem],
        cost_estimate=COST,
        compiler_params=pltpu.CompilerParams(vmem_limit_bytes=16 << 20),
        name="attend",
    )(lengths, arrived.reshape(groups, shards, 8, size), fresh, keys, values)


def output_kernel(
    where_ref, arrived_ref, facts_ref, tiles_ref, weight, out_ref, rows, total
):
    me = lax.axis_index("dp")
    slots, per_slot, tile = tiles_ref.shape[:3]
    groups, shards, capacity, columns = out_ref.shape
    places = groups * capacity
    depth, width = weight.shape
    blocks = depth // tile
    group_rows = arrived_ref.shape[0] // (groups * blocks)
    facts = facts_ref[...].astype(I32)
    own_slot = facts[:, 0:1] - 1 - me * slots
    number = facts[:, 1:2]
    home = iota((places, 1), 0) // capacity * group_rows + number - 1
    home = jnp.where(number > 0, home * blocks, -blocks)
    lane = iota((places, arrived_ref.shape[0]), 1)
    for b in range(blocks):
        gather = pick(lane == home + b).astype(BF16)
        rows[:, b * tile : (b + 1) * tile] = dot(gather, arrived_ref[...]).astype(BF16)
    total[...] = jnp.zeros_like(total)
    targets = width // tile
    for t in range(slots):
        mine = own_slot == t
        for k in range(per_slot):
            place = where_ref[t, k]
            source = pl.multiple_of((place // targets) * tile, tile)
            target = pl.multiple_of((place % targets) * tile, tile)
            product = dot(rows[:, pl.ds(source, tile)], tiles_ref[t, k])
            total[:, pl.ds(target, tile)] += jnp.where(mine, product, 0.0)
    for shard in range(shards):
        span = slice(shard * columns, (shard + 1) * columns)
        result = dot(rows[...], weight[:, span]) + total[:, span]
        out_ref[:, shard] = result.reshape(groups, capacity, columns).astype(BF16)


def output_visit(arrived, facts, tiles, where, weight, groups):
    depth, width = weight.shape
    places = facts.shape[0]
    shards = width // depth
    vmem = pl.BlockSpec(memory_space=pltpu.VMEM)
    return pl.pallas_call(
        output_kernel,
        out_shape=jax.ShapeDtypeStruct((groups, shards, places // groups, depth), BF16),
        in_specs=[
            pl.BlockSpec(memory_space=pltpu.SMEM),
            vmem,
            vmem,
            vmem,
            vmem,
        ],
        scratch_shapes=[
            pltpu.VMEM((places, depth), BF16),
            pltpu.VMEM((places, width), F32),
        ],
        cost_estimate=COST,
        compiler_params=pltpu.CompilerParams(vmem_limit_bytes=20 << 20),
        name="output_visit",
    )(where, arrived, facts, tiles, weight)


def finish_kernel(arrived_ref, place_ref, out_ref):
    stores, shards, capacity, columns = arrived_ref.shape
    total = arrived_ref[:, 0].astype(F32)
    for j in range(1, shards):
        total = total + arrived_ref[:, j].astype(F32)
    rounded = total.reshape(stores * capacity, columns).astype(BF16)
    out_ref[...] = dot(place_ref[...], rounded, ((0,), (0,))).astype(BF16)


def finish(arrived, place):
    return pl.pallas_call(
        finish_kernel,
        out_shape=jax.ShapeDtypeStruct((place.shape[1], arrived.shape[3]), BF16),
        compiler_params=pltpu.CompilerParams(vmem_limit_bytes=8 << 20),
        name="finish",
    )(arrived, place)


def swap(blocks, axes):
    return lax.all_to_all(blocks, axes, split_axis=0, concat_axis=0, tiled=True)


def body(
    activations,
    query_weight,
    output_weight,
    key_cache,
    value_cache,
    fresh_pair,
    cache_length,
    row_tenant,
    tenant_slot,
    query_deltas,
    query_where,
    output_deltas,
    output_where,
):
    groups = lax.axis_size("dp")
    shards = lax.axis_size("tensor")
    per_store = query_deltas.shape[0]
    capacity = 8
    packed, place = pack_rows(row_tenant, tenant_slot, activations, groups * capacity, per_store)
    arrived = swap(packed, "dp")
    base_query = jnp.dot(activations, query_weight, preferred_element_type=F32)
    sent_query, facts = query_visit(arrived, query_deltas, query_where, base_query, groups)
    query = swap(sent_query, EVERY)
    attended = attend(query, key_cache, value_cache, fresh_pair, cache_length, groups)
    size = attended.shape[3]
    rows = swap(attended.reshape(-1, size), EVERY)
    parts = output_visit(rows, facts, output_deltas, output_where, output_weight, groups)
    columns = parts.shape[3]
    summed = swap(parts.reshape(-1, columns), EVERY)
    return finish(summed.reshape(groups, shards, capacity, columns), place)


def solution(mesh):
    placed = (
        P("dp", None),
        P(None, "tensor"),
        P("tensor", None),
        P(("dp", "tensor"), None, None, None),
        P(("dp", "tensor"), None, None, None),
        P(("dp", "tensor"), None, None),
        P(("dp", "tensor")),
        P("dp"),
        P(),
        P("dp", "tensor", None, None),
        P("dp", "tensor"),
        P("dp", "tensor", None, None),
        P("dp", "tensor"),
    )
    return jax.shard_map(
        body, mesh=mesh, in_specs=placed, out_specs=P("dp", "tensor"), check_vma=False
    )
```

```python
import functools

import jax
import jax.numpy as jnp
from jax import lax
from jax.experimental import pallas as pl
from jax.experimental.pallas import tpu as pltpu
from jax.sharding import PartitionSpec as P

F32 = jnp.float32
BF16 = jnp.bfloat16
I32 = jnp.int32
LANES = 128
CORES = 2
EVERY = ("dp", "tensor")
COST = pl.CostEstimate(flops=1 << 35, bytes_accessed=48 << 20, transcendentals=0)


def iota(shape, axis):
    return lax.broadcasted_iota(I32, shape, axis)


def dot(a, b, contract=((1,), (0,))):
    return lax.dot_general(a, b, (contract, ((), ())), preferred_element_type=F32)


def pick(mask, value=1.0):
    return jnp.where(mask, value, 0.0)


def pack_kernel(
    per_store, tenant_hbm, slot_hbm, rows_hbm, out_hbm, place_ref, tenant_ref, slot_ref, rows, out, sems
):
    group = lax.axis_index("dp")
    core = lax.axis_index("tensor") % CORES
    count, width = rows.shape
    tenants = slot_ref.shape[1]
    places = out.shape[0]
    capacity = 8
    stores = places // capacity
    chunks = sems.shape[1] - 2
    step = width // chunks

    def load(n):
        source = pl.ds(pl.multiple_of(core * width + n * step, LANES), step)
        target = pl.ds(n * step, step)
        return pltpu.make_async_copy(rows_hbm.at[:, source], rows.at[:, target], sems.at[0, n])

    def store_out(n):
        span = pl.ds(n * step, step if n < chunks else 2 * LANES)
        return pltpu.make_async_copy(out.at[:, span], out_hbm.at[:, span], sems.at[1, n])

    small = (
        pltpu.make_async_copy(tenant_hbm, tenant_ref, sems.at[0, chunks]),
        pltpu.make_async_copy(slot_hbm, slot_ref, sems.at[0, chunks + 1]),
    )
    for copy in small:
        copy.start()
    for n in range(chunks):
        load(n).start()
    for copy in small:
        copy.wait()
    chosen = pick(iota((tenants, count), 0) == tenant_ref[...]).astype(BF16)
    table = jnp.broadcast_to(slot_ref[...].astype(F32), (8, tenants)).astype(BF16)
    slot = dot(table, chosen)[0:1].astype(I32)
    store = slot // per_store
    at_store = pick(iota((stores, count), 0) == store)
    earlier = pick(iota((count, count), 0) < iota((count, count), 1)).astype(BF16)
    before = dot(at_store.astype(BF16), earlier)
    rank = jnp.sum(at_store * before, axis=0, keepdims=True).astype(I32)
    placed = iota((places, count), 0) == store * capacity + rank
    hot = pick(placed).astype(BF16)
    place_ref[...] = hot
    for n in range(chunks):
        load(n).wait()
        span = slice(n * step, (n + 1) * step)
        out[:, span] = dot(hot, rows[:, span]).astype(BF16)
        store_out(n).start()
    number = iota((1, count), 1) + 1
    lane_of = iota((LANES, count), 0) % (LANES // 2)
    spread = jnp.where(lane_of == group * capacity + rank, number, 0).astype(F32).astype(BF16)
    by_lane = dot(at_store.astype(BF16), spread, ((1,), (1,)))
    wide = jnp.broadcast_to(by_lane[:, None, :], (stores, capacity, LANES))
    out[:, width : width + LANES] = wide.reshape(places, LANES).astype(BF16)
    slot_col = jnp.sum(jnp.where(placed, slot + 1, 0).astype(F32), axis=1, keepdims=True)
    row_col = jnp.sum(jnp.where(placed, number, 0).astype(F32), axis=1, keepdims=True)
    lane = iota((places, LANES), 1)
    facts = jnp.where(lane == 0, slot_col, jnp.where(lane == 1, row_col, 0.0))
    out[:, width + LANES : width + 2 * LANES] = facts.astype(BF16)
    store_out(chunks).start()
    for n in range(chunks + 1):
        store_out(n).wait()


def in_hbm(array):
    return pltpu.with_memory_space_constraint(array, pltpu.HBM)


def pack_rows(row_tenant, tenant_slot, rows, places, per_store):
    count, width = rows.shape
    half = width // CORES
    chunks = 4
    hbm = pl.BlockSpec(memory_space=pltpu.HBM)
    return pl.pallas_call(
        functools.partial(pack_kernel, per_store),
        out_shape=(
            jax.ShapeDtypeStruct((places, half + 2 * LANES), BF16),
            jax.ShapeDtypeStruct((places, count), BF16),
        ),
        in_specs=[hbm, hbm, hbm],
        out_specs=(hbm, pl.BlockSpec(memory_space=pltpu.VMEM)),
        scratch_shapes=[
            pltpu.VMEM((1, count), I32),
            pltpu.VMEM((1, tenant_slot.shape[0]), I32),
            pltpu.VMEM((count, half), BF16),
            pltpu.VMEM((places, half + 2 * LANES), BF16),
            pltpu.SemaphoreType.DMA((2, chunks + 2)),
        ],
        compiler_params=pltpu.CompilerParams(vmem_limit_bytes=4 << 20),
        name="pack_rows",
    )(
        in_hbm(row_tenant.reshape(1, count)), in_hbm(tenant_slot.reshape(1, -1)), in_hbm(rows)
    )


def query_kernel(where_ref, mine_ref, other_ref, tiles_ref, base_ref, out_ref, facts_ref, total):
    me = lax.axis_index("dp")
    core = lax.axis_index("tensor") % CORES
    slots, per_slot, tile = tiles_ref.shape[:3]
    places = mine_ref.shape[0]
    width = mine_ref.shape[1] - 2 * LANES
    blocks = total.shape[1] // tile
    halves = width // tile
    group_rows = base_ref.shape[0] // blocks
    groups = out_ref.shape[0] // base_ref.shape[0]
    capacity = places // groups
    facts = mine_ref[:, width + LANES : width + 2 * LANES].astype(F32)
    facts_ref[...] = facts
    own_slot = facts[:, 0:1].astype(I32) - 1 - me * slots
    total[...] = jnp.zeros_like(total)
    for t in range(slots):
        mine = own_slot == t
        for k in range(per_slot):
            place = where_ref[t, k]
            source = place // blocks
            span = pl.ds(pl.multiple_of(source % halves * tile, tile), tile)
            target = pl.multiple_of(place % blocks * tile, tile)
            rows = jnp.where(source // halves == core, mine_ref[:, span], other_ref[:, span])
            product = dot(rows, tiles_ref[t, k])
            total[:, pl.ds(target, tile)] += jnp.where(mine, product, 0.0)
    stacked = jnp.concatenate(
        [total[:, b * tile : (b + 1) * tile] for b in range(blocks)], axis=0
    ).astype(BF16)
    by_lane = mine_ref[:, width : width + LANES].astype(F32)
    by_lane = jnp.sum(by_lane.reshape(groups, capacity, LANES), axis=0)[0:1].astype(I32)
    lane = iota((1, LANES), 1)
    home = (lane % places) // capacity * group_rows + by_lane - 1
    home = jnp.where(by_lane > 0, home * blocks + lane // places, -blocks)
    block_rows = group_rows * blocks
    for g in range(groups):
        row = iota((block_rows, LANES), 0) + g * block_rows
        expand = jnp.concatenate(
            [pick(row == home + b).astype(BF16) for b in range(0, blocks, LANES // places)],
            axis=1,
        )
        sent = dot(expand, stacked) + jnp.where(me == g, base_ref[...], 0.0)
        out_ref[g * block_rows : (g + 1) * block_rows, :] = sent.astype(BF16)


def query_visit(mine, other, tiles, where, base, groups):
    places = mine.shape[0]
    tile = tiles.shape[2]
    columns = base.shape[1]
    blocks = columns // tile
    stacked = base.reshape(base.shape[0] * blocks, tile)
    vmem = pl.BlockSpec(memory_space=pltpu.VMEM)
    return pl.pallas_call(
        query_kernel,
        out_shape=(
            jax.ShapeDtypeStruct((groups * stacked.shape[0], tile), BF16),
            jax.ShapeDtypeStruct((places, LANES), F32),
        ),
        in_specs=[pl.BlockSpec(memory_space=pltpu.SMEM), vmem, vmem, vmem, vmem],
        scratch_shapes=[pltpu.VMEM((places, columns), F32)],
        cost_estimate=COST,
        compiler_params=pltpu.CompilerParams(vmem_limit_bytes=12 << 20),
        name="query_visit",
    )(where, mine, other, tiles, stacked)


def attend_kernel(
    length_ref, arrived_ref, fresh_ref, keys, values, out_ref
):
    requests, kv_heads, context, size = keys.shape
    shards = out_ref.shape[1]
    stores = arrived_ref.shape[0]
    scale = size ** (-0.5)
    query = arrived_ref[0].astype(F32)
    for s in range(1, stores):
        query = query + arrived_ref[s].astype(F32)
    fresh = fresh_ref[...].astype(F32)
    upper = iota((8, size), 0) < 4
    position = iota((1, context), 1)
    mixed = [[None] * kv_heads for _ in range(requests)]
    for i in range(requests):
        visible = position < length_ref[i]
        parts = []
        for g in range(kv_heads):
            first, second = query[2 * g], query[2 * g + 1]
            if i == 0:
                heads = jnp.where(upper, first, pltpu.roll(second, 4, 0))
            else:
                heads = jnp.where(upper, pltpu.roll(first, 4, 0), second)
            heads = heads.astype(BF16)
            scores = dot(heads, keys[i, g], ((1,), (1,))) * scale
            fresh_key = fresh[i, 0:1, g * size : (g + 1) * size]
            own = jnp.sum(heads.astype(F32) * fresh_key, axis=1, keepdims=True) * scale
            scores = jnp.where(visible, scores, -1e30)
            highest = jnp.maximum(jnp.max(scores, axis=1, keepdims=True), own)
            weights = jnp.where(visible, jnp.exp(scores - highest), 0.0)
            own_weight = jnp.exp(own - highest)
            total = jnp.sum(weights, axis=1, keepdims=True) + own_weight
            share = (weights / total).astype(BF16)
            own_share = (own_weight / total).astype(BF16).astype(F32)
            parts.append((share, own_share))
        for g in range(kv_heads):
            share, own_share = parts[g]
            fresh_value = fresh[i, 1:2, g * size : (g + 1) * size]
            mixed[i][g] = dot(share, values[i, g]) + own_share * fresh_value
    for g in range(kv_heads):
        one, two = mixed[0][g], mixed[1][g]
        first = jnp.where(upper, one, pltpu.roll(two, 4, 0)).astype(BF16)
        second = jnp.where(upper, pltpu.roll(one, 4, 0), two).astype(BF16)
        for d in range(out_ref.shape[0]):
            out_ref[d, 2 * g] = first
            out_ref[d, 2 * g + 1] = second


def attend(arrived, keys, values, fresh, lengths, groups):
    requests, kv_heads, context, size = keys.shape
    shards = arrived.shape[0] // (groups * 8)
    vmem = pl.BlockSpec(memory_space=pltpu.VMEM)
    return pl.pallas_call(
        attend_kernel,
        out_shape=jax.ShapeDtypeStruct((groups, shards, 8, size), BF16),
        in_specs=[pl.BlockSpec(memory_space=pltpu.SMEM), vmem, vmem, vmem, vmem],
        cost_estimate=COST,
        compiler_params=pltpu.CompilerParams(vmem_limit_bytes=16 << 20),
        name="attend",
    )(lengths, arrived.reshape(groups, shards, 8, size), fresh, keys, values)


def output_kernel(
    where_ref, arrived_ref, facts_ref, tiles_ref, weight, out_ref, rows_ref, total_ref
):
    me = lax.axis_index("dp")
    other = 1 - lax.axis_index("tensor") % CORES
    slots, per_slot, tile = tiles_ref.shape[:3]
    groups, shards, capacity, columns = out_ref.shape
    places = groups * capacity
    depth, width = weight.shape
    blocks = depth // tile
    group_rows = arrived_ref.shape[0] // (groups * blocks)
    facts = facts_ref[...].astype(I32)
    own_slot = facts[:, 0:1] - 1 - me * slots
    number = facts[:, 1:2]
    home = iota((places, 1), 0) // capacity * group_rows + number - 1
    home = jnp.where(number > 0, home * blocks, -blocks)
    lane = iota((places, arrived_ref.shape[0]), 1)
    for b in range(blocks):
        gather = pick(lane == home + b).astype(BF16)
        rows_ref[:, b * tile : (b + 1) * tile] = dot(gather, arrived_ref[...]).astype(BF16)
    total_ref[...] = jnp.zeros_like(total_ref)
    targets = width // tile
    for t in range(slots):
        mine = own_slot == t
        for k in range(per_slot):
            place = where_ref[t, k]
            source = pl.multiple_of(place // targets * tile, tile)
            target = pl.multiple_of(place % targets * tile, tile)
            product = dot(rows_ref[:, pl.ds(source, tile)], tiles_ref[t, k])
            total_ref[:, pl.ds(target, tile)] += jnp.where(mine, product, 0.0)
    add_base(other, rows_ref, weight, total_ref, out_ref)


def add_base(half, rows_ref, weight, total_ref, out_ref):
    groups, shards, capacity, columns = out_ref.shape
    for shard in range(shards):
        start = (shard * CORES + half) * columns
        span = pl.ds(pl.multiple_of(start, columns), columns)
        result = dot(rows_ref[...], weight[:, span]) + total_ref[:, span]
        out_ref[:, shard] = result.reshape(groups, capacity, columns).astype(out_ref.dtype)


def output_visit(arrived, facts, tiles, where, weight, groups):
    depth, width = weight.shape
    places = facts.shape[0]
    shards = width // depth
    vmem = pl.BlockSpec(memory_space=pltpu.VMEM)
    return pl.pallas_call(
        output_kernel,
        out_shape=(
            jax.ShapeDtypeStruct((groups, shards, places // groups, depth // CORES), BF16),
            jax.ShapeDtypeStruct((places, depth), BF16),
            jax.ShapeDtypeStruct((places, width), F32),
        ),
        in_specs=[pl.BlockSpec(memory_space=pltpu.SMEM), vmem, vmem, vmem, vmem],
        out_specs=(vmem, vmem, vmem),
        cost_estimate=COST,
        compiler_params=pltpu.CompilerParams(vmem_limit_bytes=16 << 20),
        name="output_visit",
    )(where, arrived, facts, tiles, weight)


def own_kernel(rows_ref, weight, total_ref, out_ref):
    add_base(lax.axis_index("tensor") % CORES, rows_ref, weight, total_ref, out_ref)


def output_own(rows, weight, total, shape):
    vmem = pl.BlockSpec(memory_space=pltpu.VMEM)
    return pl.pallas_call(
        own_kernel,
        out_shape=jax.ShapeDtypeStruct(shape, F32),
        in_specs=[vmem, vmem, vmem],
        out_specs=vmem,
        cost_estimate=COST,
        compiler_params=pltpu.CompilerParams(vmem_limit_bytes=16 << 20),
        name="output_own",
    )(rows, weight, total)


def finish_kernel(arrived_ref, place_ref, out_ref):
    stores, pairs, cores, capacity, columns = arrived_ref.shape
    for core in range(cores):
        total = arrived_ref[:, 0, core].astype(F32)
        for pair in range(1, pairs):
            total = total + arrived_ref[:, pair, core].astype(F32)
        rounded = total.reshape(stores * capacity, columns).astype(BF16)
        span = slice(core * columns, (core + 1) * columns)
        out_ref[:, span] = dot(place_ref[...], rounded, ((0,), (0,))).astype(BF16)


def finish(arrived, place):
    cores, columns = arrived.shape[2], arrived.shape[4]
    return pl.pallas_call(
        finish_kernel,
        out_shape=jax.ShapeDtypeStruct((place.shape[1], cores * columns), BF16),
        compiler_params=pltpu.CompilerParams(vmem_limit_bytes=8 << 20),
        name="finish",
    )(arrived, place)


def across_chip(block):
    count = lax.axis_size("tensor")
    return lax.ppermute(block, "tensor", [(i, i ^ 1) for i in range(count)])


def swap(blocks, axes):
    return lax.all_to_all(blocks, axes, split_axis=0, concat_axis=0, tiled=True)


def body(
    activations,
    query_weight,
    output_weight,
    key_cache,
    value_cache,
    fresh_pair,
    cache_length,
    row_tenant,
    tenant_slot,
    query_deltas,
    query_where,
    output_deltas,
    output_where,
):
    groups = lax.axis_size("dp")
    shards = lax.axis_size("tensor")
    per_store = query_deltas.shape[0]
    capacity = 8
    packed, place = pack_rows(row_tenant, tenant_slot, activations, groups * capacity, per_store)
    arrived = swap(packed.reshape(groups, capacity, -1), "dp").reshape(packed.shape)
    base_query = jnp.dot(activations, query_weight, preferred_element_type=F32)
    arrived, base_query = lax.optimization_barrier((arrived, base_query))
    other = across_chip(arrived)
    sent_query, facts = query_visit(
        arrived, other, query_deltas, query_where, base_query, groups
    )
    query = swap(sent_query, EVERY)
    attended = attend(query, key_cache, value_cache, fresh_pair, cache_length, groups)
    size = attended.shape[3]
    rows = swap(attended.reshape(-1, size), EVERY)
    sent, visitors, delta = output_visit(
        rows, facts, output_deltas, output_where, output_weight, groups
    )
    received = across_chip(sent)
    own = output_own(visitors, output_weight, delta, sent.shape)
    parts = (own + received.astype(F32)).astype(BF16)
    columns = parts.shape[3]
    summed = swap(parts.reshape(-1, columns), EVERY)
    return finish(summed.reshape(groups, shards // CORES, CORES, capacity, columns), place)


def solution(mesh):
    placed = (
        P("dp", None),
        P(None, "tensor"),
        P("tensor", None),
        P(("dp", "tensor"), None, None, None),
        P(("dp", "tensor"), None, None, None),
        P(("dp", "tensor"), None, None),
        P(("dp", "tensor")),
        P("dp"),
        P(),
        P("dp", "tensor", None, None),
        P("dp", "tensor"),
        P("dp", "tensor", None, None),
        P("dp", "tensor"),
    )
    return jax.shard_map(
        body, mesh=mesh, in_specs=placed, out_specs=P("dp", "tensor"), check_vma=False
    )
```

```python
import functools

import jax
import jax.numpy as jnp
from jax import lax
from jax.experimental import pallas as pl
from jax.experimental.pallas import tpu as pltpu
from jax.sharding import PartitionSpec as P

F32 = jnp.float32
BF16 = jnp.bfloat16
I32 = jnp.int32
LANES = 128
CORES = 2
EVERY = ("dp", "tensor")
COST = pl.CostEstimate(flops=1 << 35, bytes_accessed=48 << 20, transcendentals=0)


def iota(shape, axis):
    return lax.broadcasted_iota(I32, shape, axis)


def dot(a, b, contract=((1,), (0,))):
    return lax.dot_general(a, b, (contract, ((), ())), preferred_element_type=F32)


def log2(size):
    return size.bit_length() - 1


def pick(mask, value=1.0):
    return jnp.where(mask, value, 0.0)


def pack_kernel(
    per_store, tenant_hbm, slot_hbm, rows_hbm, out, place_ref, tenant_ref, slot_ref, rows, sems
):
    group = lax.axis_index("dp")
    core = lax.axis_index("tensor") % CORES
    count, width = rows.shape
    tenants = slot_ref.shape[1]
    places = out.shape[0]
    capacity = 8
    stores = places // capacity
    chunks = sems.shape[0] - 2
    step = width // chunks

    def load(n):
        source = pl.ds(pl.multiple_of(core * width + n * step, LANES), step)
        target = pl.ds(n * step, step)
        return pltpu.make_async_copy(rows_hbm.at[:, source], rows.at[:, target], sems.at[n])

    small = (
        pltpu.make_async_copy(tenant_hbm, tenant_ref, sems.at[chunks]),
        pltpu.make_async_copy(slot_hbm, slot_ref, sems.at[chunks + 1]),
    )
    for copy in small:
        copy.start()
    for n in range(chunks):
        load(n).start()
    for copy in small:
        copy.wait()
    chosen = pick(iota((tenants, count), 0) == tenant_ref[...]).astype(BF16)
    table = jnp.broadcast_to(slot_ref[...].astype(F32), (8, tenants)).astype(BF16)
    slot = dot(table, chosen)[0:1].astype(I32)
    store = slot // per_store
    at_store = pick(iota((stores, count), 0) == store)
    earlier = pick(iota((count, count), 0) < iota((count, count), 1)).astype(BF16)
    before = dot(at_store.astype(BF16), earlier)
    rank = jnp.sum(at_store * before, axis=0, keepdims=True).astype(I32)
    placed = iota((places, count), 0) == store * capacity + rank
    hot = pick(placed).astype(BF16)
    place_ref[...] = hot
    for n in range(chunks):
        load(n).wait()
        span = slice(n * step, (n + 1) * step)
        out[:, span] = dot(hot, rows[:, span]).astype(BF16)
    number = iota((1, count), 1) + 1
    lane_of = iota((LANES, count), 0) % (LANES // 2)
    spread = jnp.where(lane_of == group * capacity + rank, number, 0).astype(F32).astype(BF16)
    by_lane = dot(at_store.astype(BF16), spread, ((1,), (1,)))
    wide = jnp.broadcast_to(by_lane[:, None, :], (stores, capacity, LANES))
    out[:, width : width + LANES] = wide.reshape(places, LANES).astype(BF16)
    slot_col = jnp.sum(jnp.where(placed, slot + 1, 0).astype(F32), axis=1, keepdims=True)
    row_col = jnp.sum(jnp.where(placed, number, 0).astype(F32), axis=1, keepdims=True)
    lane = iota((places, LANES), 1)
    facts = jnp.where(lane == 0, slot_col, jnp.where(lane == 1, row_col, 0.0))
    out[:, width + LANES : width + 2 * LANES] = facts.astype(BF16)


def in_hbm(array):
    return pltpu.with_memory_space_constraint(array, pltpu.HBM)


def pack_rows(row_tenant, tenant_slot, rows, places, per_store):
    count, width = rows.shape
    half = width // CORES
    chunks = 4
    hbm = pl.BlockSpec(memory_space=pltpu.HBM)
    vmem = pl.BlockSpec(memory_space=pltpu.VMEM)
    return pl.pallas_call(
        functools.partial(pack_kernel, per_store),
        out_shape=(
            jax.ShapeDtypeStruct((places, half + 2 * LANES), BF16),
            jax.ShapeDtypeStruct((places, count), BF16),
        ),
        in_specs=[hbm, hbm, hbm],
        out_specs=(vmem, vmem),
        scratch_shapes=[
            pltpu.VMEM((1, count), I32),
            pltpu.VMEM((1, tenant_slot.shape[0]), I32),
            pltpu.VMEM((count, half), BF16),
            pltpu.SemaphoreType.DMA((chunks + 2,)),
        ],
        cost_estimate=COST,
        compiler_params=pltpu.CompilerParams(vmem_limit_bytes=4 << 20),
        name="pack_rows",
    )(
        in_hbm(row_tenant.reshape(1, count)), in_hbm(tenant_slot.reshape(1, -1)), in_hbm(rows)
    )


def query_kernel(
    group_rows, where_vmem, mine_ref, other_ref, tiles_ref, base_ref, out_ref, facts_ref, where_ref, sem, expand, *totals
):
    fetch = pltpu.make_async_copy(where_vmem, where_ref, sem)
    fetch.start()
    me = lax.axis_index("dp")
    core = lax.axis_index("tensor") % CORES
    slots, per_slot, tile = tiles_ref.shape[:3]
    places = mine_ref.shape[0]
    width = mine_ref.shape[1] - 2 * LANES
    halves = width // tile
    groups = lax.axis_size("dp")
    blocks = base_ref.shape[0] // group_rows
    capacity = places // groups
    facts = mine_ref[:, width + LANES : width + 2 * LANES].astype(F32)
    facts_ref[...] = facts
    own_slot = facts[:, 0:1].astype(I32) - 1 - me * slots
    by_lane = mine_ref[:, width : width + LANES].astype(F32)
    by_lane = jnp.sum(by_lane.reshape(groups, capacity, LANES), axis=0)[0:1].astype(I32)
    lane = iota((1, LANES), 1)
    home = (lane % places) // capacity * group_rows + by_lane - 1
    home = jnp.where(by_lane > 0, home * blocks + lane // places, -blocks)
    block_rows = group_rows * blocks
    for g in range(groups):
        row = iota((block_rows, LANES), 0) + g * block_rows
        for n, b in enumerate(range(0, blocks, LANES // places)):
            one_hot = pick(row == home + b).astype(BF16)
            expand[g * block_rows : (g + 1) * block_rows, n * LANES : (n + 1) * LANES] = one_hot
    for total in totals:
        total[...] = jnp.zeros_like(total)
    fetch.wait()
    for t in range(slots):
        mine = own_slot == t
        for k in range(per_slot):
            place = where_ref[t, k]
            source = lax.shift_right_logical(place, log2(blocks))
            start = lax.shift_left(source & (halves - 1), log2(tile))
            target = lax.shift_left(place & (blocks - 1), log2(tile))
            span = pl.ds(pl.multiple_of(start, tile), tile)
            own_half = lax.shift_right_logical(source, log2(halves)) == core
            rows = jnp.where(own_half, mine_ref[:, span], other_ref[:, span])
            product = dot(rows, tiles_ref[t, k])
            total = totals[k % len(totals)]
            total[:, pl.ds(pl.multiple_of(target, tile), tile)] += jnp.where(mine, product, 0.0)
    whole = totals[0][...]
    for total in totals[1:]:
        whole = whole + total[...]
    sums = [whole[:, b * tile : (b + 1) * tile] for b in range(blocks)]
    stacked = jnp.concatenate(sums, axis=0).astype(BF16)
    for g in range(groups):
        span = slice(g * block_rows, (g + 1) * block_rows)
        sent = dot(expand[span, :], stacked) + jnp.where(me == g, base_ref[...], 0.0)
        out_ref[span, :] = sent.astype(BF16)


def query_visit(mine, other, tiles, where, base, groups):
    places = mine.shape[0]
    tile = tiles.shape[2]
    columns = base.shape[1]
    blocks = columns // tile
    stacked = base.reshape(base.shape[0] * blocks, tile)
    vmem = pl.BlockSpec(memory_space=pltpu.VMEM)
    return pl.pallas_call(
        functools.partial(query_kernel, base.shape[0]),
        out_shape=(
            jax.ShapeDtypeStruct((groups * stacked.shape[0], tile), BF16),
            jax.ShapeDtypeStruct((places, LANES), F32),
        ),
        in_specs=[vmem] * 5,
        scratch_shapes=[
            pltpu.SMEM(where.shape, I32),
            pltpu.SemaphoreType.DMA,
            pltpu.VMEM((groups * stacked.shape[0], places * blocks), BF16),
        ]
        + [pltpu.VMEM((places, columns), F32)] * 4,
        cost_estimate=COST,
        compiler_params=pltpu.CompilerParams(vmem_limit_bytes=12 << 20),
        name="query_visit",
    )(where, mine, other, tiles, stacked)


def attend_kernel(
    length_vmem, arrived_ref, fresh_ref, keys, values, out_ref, length_ref, sem
):
    fetch = pltpu.make_async_copy(length_vmem, length_ref, sem)
    fetch.start()
    requests, kv_heads, context, size = keys.shape
    shards = out_ref.shape[1]
    stores = arrived_ref.shape[0]
    scale = size ** (-0.5)
    query = arrived_ref[0].astype(F32)
    for s in range(1, stores):
        query = query + arrived_ref[s].astype(F32)
    fresh = fresh_ref[...].astype(F32)
    upper = iota((8, size), 0) < 4
    position = iota((1, context), 1)
    fetch.wait()
    mixed = [[None] * kv_heads for _ in range(requests)]
    for i in range(requests):
        visible = position < length_ref[i]
        parts = []
        for g in range(kv_heads):
            first, second = query[2 * g], query[2 * g + 1]
            if i == 0:
                heads = jnp.where(upper, first, pltpu.roll(second, 4, 0))
            else:
                heads = jnp.where(upper, pltpu.roll(first, 4, 0), second)
            heads = heads.astype(BF16)
            scores = dot(heads, keys[i, g], ((1,), (1,))) * scale
            fresh_key = fresh[i, 0:1, g * size : (g + 1) * size]
            own = jnp.sum(heads.astype(F32) * fresh_key, axis=1, keepdims=True) * scale
            scores = jnp.where(visible, scores, -1e30)
            highest = jnp.maximum(jnp.max(scores, axis=1, keepdims=True), own)
            weights = jnp.where(visible, jnp.exp(scores - highest), 0.0)
            own_weight = jnp.exp(own - highest)
            total = jnp.sum(weights, axis=1, keepdims=True) + own_weight
            share = (weights / total).astype(BF16)
            own_share = (own_weight / total).astype(BF16).astype(F32)
            parts.append((share, own_share))
        for g in range(kv_heads):
            share, own_share = parts[g]
            fresh_value = fresh[i, 1:2, g * size : (g + 1) * size]
            mixed[i][g] = dot(share, values[i, g]) + own_share * fresh_value
    for g in range(kv_heads):
        one, two = mixed[0][g], mixed[1][g]
        first = jnp.where(upper, one, pltpu.roll(two, 4, 0)).astype(BF16)
        second = jnp.where(upper, pltpu.roll(one, 4, 0), two).astype(BF16)
        for d in range(out_ref.shape[0]):
            out_ref[d, 2 * g] = first
            out_ref[d, 2 * g + 1] = second


def attend(arrived, keys, values, fresh, lengths, groups):
    requests, kv_heads, context, size = keys.shape
    shards = arrived.shape[0] // (groups * 8)
    vmem = pl.BlockSpec(memory_space=pltpu.VMEM)
    return pl.pallas_call(
        attend_kernel,
        out_shape=jax.ShapeDtypeStruct((groups, shards, 8, size), BF16),
        in_specs=[vmem] * 5,
        scratch_shapes=[pltpu.SMEM(lengths.shape, I32), pltpu.SemaphoreType.DMA],
        cost_estimate=COST,
        compiler_params=pltpu.CompilerParams(vmem_limit_bytes=16 << 20),
        name="attend",
    )(lengths, arrived.reshape(groups, shards, 8, size), fresh, keys, values)


def output_kernel(
    where_vmem, arrived_ref, facts_ref, tiles_ref, weight, out_ref, rows_ref, total_ref, where_ref, sem, hold
):
    fetch = pltpu.make_async_copy(where_vmem, where_ref, sem)
    fetch.start()
    me = lax.axis_index("dp")
    other = 1 - lax.axis_index("tensor") % CORES
    slots, per_slot, tile = tiles_ref.shape[:3]
    groups, shards, capacity, columns = out_ref.shape
    places = groups * capacity
    depth, width = weight.shape
    blocks = depth // tile
    group_rows = arrived_ref.shape[0] // (groups * blocks)
    facts = facts_ref[...].astype(I32)
    own_slot = facts[:, 0:1] - 1 - me * slots
    number = facts[:, 1:2]
    home = iota((places, 1), 0) // capacity * group_rows + number - 1
    home = jnp.where(number > 0, home * blocks, -blocks)
    total_ref[...] = jnp.zeros_like(total_ref)
    lane = iota((places, arrived_ref.shape[0]), 1)
    gather = jnp.concatenate([pick(lane == home + b).astype(BF16) for b in range(blocks)], axis=0)
    gathered = dot(gather, arrived_ref[...]).astype(BF16)
    for b in range(blocks):
        rows_ref[:, b * tile : (b + 1) * tile] = gathered[b * places : (b + 1) * places]
    targets = width // tile
    fetch.wait()
    every = slots * per_slot // shards
    for shard in range(shards):
        for n in range(shard * every, (shard + 1) * every):
            t, k = n // per_slot, n % per_slot
            place = where_ref[t, k]
            source = lax.shift_left(lax.shift_right_logical(place, log2(targets)), log2(tile))
            target = lax.shift_left(place & (targets - 1), log2(tile))
            rows = rows_ref[:, pl.ds(pl.multiple_of(source, tile), tile)]
            product = dot(rows, tiles_ref[t, k])
            span = pl.ds(pl.multiple_of(target, tile), tile)
            total_ref[:, span] += jnp.where(own_slot == t, product, 0.0)
        hold[shard] = dot(rows_ref[...], weight[:, columns_of(shard, other, columns)])
    for shard in range(shards):
        result = hold[shard] + total_ref[:, columns_of(shard, other, columns)]
        out_ref[:, shard] = result.reshape(groups, capacity, columns).astype(BF16)


def columns_of(shard, half, columns):
    return pl.ds(pl.multiple_of((shard * CORES + half) * columns, columns), columns)


def output_visit(arrived, facts, tiles, where, weight, groups):
    depth, width = weight.shape
    places = facts.shape[0]
    shards = width // depth
    vmem = pl.BlockSpec(memory_space=pltpu.VMEM)
    return pl.pallas_call(
        output_kernel,
        out_shape=(
            jax.ShapeDtypeStruct((groups, shards, places // groups, depth // CORES), BF16),
            jax.ShapeDtypeStruct((places, depth), BF16),
            jax.ShapeDtypeStruct((places, width), F32),
        ),
        in_specs=[vmem] * 5,
        out_specs=(vmem, vmem, vmem),
        scratch_shapes=[pltpu.SMEM(where.shape, I32), pltpu.SemaphoreType.DMA, pltpu.VMEM((shards, places, depth // CORES), F32)],
        cost_estimate=COST,
        compiler_params=pltpu.CompilerParams(vmem_limit_bytes=16 << 20),
        name="output_visit",
    )(where, arrived, facts, tiles, weight)


def own_kernel(rows_ref, weight, total_ref, out_ref):
    core = lax.axis_index("tensor") % CORES
    groups, shards, capacity, columns = out_ref.shape
    for shard in range(shards):
        span = columns_of(shard, core, columns)
        result = dot(rows_ref[...], weight[:, span]) + total_ref[:, span]
        out_ref[:, shard] = result.reshape(groups, capacity, columns)


def output_own(rows, weight, total, shape):
    vmem = pl.BlockSpec(memory_space=pltpu.VMEM)
    return pl.pallas_call(
        own_kernel,
        out_shape=jax.ShapeDtypeStruct(shape, F32),
        in_specs=[vmem, vmem, vmem],
        out_specs=vmem,
        cost_estimate=COST,
        compiler_params=pltpu.CompilerParams(vmem_limit_bytes=16 << 20),
        name="output_own",
    )(rows, weight, total)


def finish_kernel(arrived_ref, place_ref, out_ref):
    stores, pairs, cores, capacity, columns = arrived_ref.shape
    for core in range(cores):
        total = arrived_ref[:, 0, core].astype(F32)
        for pair in range(1, pairs):
            total = total + arrived_ref[:, pair, core].astype(F32)
        rounded = total.reshape(stores * capacity, columns).astype(BF16)
        span = slice(core * columns, (core + 1) * columns)
        out_ref[:, span] = dot(place_ref[...], rounded, ((0,), (0,))).astype(BF16)


def finish(arrived, place):
    cores, columns = arrived.shape[2], arrived.shape[4]
    return pl.pallas_call(
        finish_kernel,
        out_shape=jax.ShapeDtypeStruct((place.shape[1], cores * columns), BF16),
        compiler_params=pltpu.CompilerParams(vmem_limit_bytes=8 << 20),
        name="finish",
    )(arrived, place)


def across_chip(block):
    count = lax.axis_size("tensor")
    return lax.ppermute(block, "tensor", [(i, i ^ 1) for i in range(count)])


def swap(blocks, axes):
    return lax.all_to_all(blocks, axes, split_axis=0, concat_axis=0, tiled=True)


def body(
    activations,
    query_weight,
    output_weight,
    key_cache,
    value_cache,
    fresh_pair,
    cache_length,
    row_tenant,
    tenant_slot,
    query_deltas,
    query_where,
    output_deltas,
    output_where,
):
    groups = lax.axis_size("dp")
    shards = lax.axis_size("tensor")
    per_store = query_deltas.shape[0]
    capacity = 8
    packed, place = pack_rows(row_tenant, tenant_slot, activations, groups * capacity, per_store)
    arrived = swap(packed.reshape(groups, capacity, -1), "dp").reshape(packed.shape)
    base_query = jnp.dot(activations, query_weight, preferred_element_type=F32)
    other = across_chip(arrived)
    sent_query, facts = query_visit(
        arrived, other, query_deltas, query_where, base_query, groups
    )
    query = swap(sent_query, EVERY)
    attended = attend(query, key_cache, value_cache, fresh_pair, cache_length, groups)
    size = attended.shape[3]
    rows = swap(attended.reshape(-1, size), EVERY)
    sent, visitors, delta = output_visit(
        rows, facts, output_deltas, output_where, output_weight, groups
    )
    received = across_chip(sent)
    own = output_own(visitors, output_weight, delta, sent.shape)
    parts = (own + received.astype(F32)).astype(BF16)
    columns = parts.shape[3]
    summed = swap(parts.reshape(-1, columns), EVERY)
    return finish(summed.reshape(groups, shards // CORES, CORES, capacity, columns), place)


def solution(mesh):
    placed = (
        P("dp", None),
        P(None, "tensor"),
        P("tensor", None),
        P(("dp", "tensor"), None, None, None),
        P(("dp", "tensor"), None, None, None),
        P(("dp", "tensor"), None, None),
        P(("dp", "tensor")),
        P("dp"),
        P(),
        P("dp", "tensor", None, None),
        P("dp", "tensor"),
        P("dp", "tensor", None, None),
        P("dp", "tensor"),
    )
    return jax.shard_map(
        body, mesh=mesh, in_specs=placed, out_specs=P("dp", "tensor"), check_vma=False
    )
```

```python
import functools

import jax
import jax.numpy as jnp
from jax import lax
from jax.experimental import pallas as pl
from jax.experimental.pallas import tpu as pltpu
from jax.sharding import PartitionSpec as P

F32 = jnp.float32
BF16 = jnp.bfloat16
I32 = jnp.int32
LANES = 128
CORES = 2
EVERY = ("dp", "tensor")
COST = pl.CostEstimate(flops=1 << 35, bytes_accessed=48 << 20, transcendentals=0)


def iota(shape, axis):
    return lax.broadcasted_iota(I32, shape, axis)


def dot(a, b, contract=((1,), (0,))):
    return lax.dot_general(a, b, (contract, ((), ())), preferred_element_type=F32)


def log2(size):
    return size.bit_length() - 1


def pick(mask, value=1.0):
    return jnp.where(mask, value, 0.0)


def pack_kernel(
    per_store, tenant_hbm, slot_hbm, rows_hbm, out, place_ref, tenant_ref, slot_ref, rows, sems
):
    group = lax.axis_index("dp")
    core = lax.axis_index("tensor") % CORES
    count, width = rows.shape
    tenants = slot_ref.shape[1]
    places = out.shape[0]
    capacity = 8
    stores = places // capacity
    chunks = sems.shape[0] - 2
    step = width // chunks

    def load(n):
        source = pl.ds(pl.multiple_of(core * width + n * step, LANES), step)
        target = pl.ds(n * step, step)
        return pltpu.make_async_copy(rows_hbm.at[:, source], rows.at[:, target], sems.at[n])

    small = (
        pltpu.make_async_copy(tenant_hbm, tenant_ref, sems.at[chunks]),
        pltpu.make_async_copy(slot_hbm, slot_ref, sems.at[chunks + 1]),
    )
    for copy in small:
        copy.start()
    for n in range(chunks):
        load(n).start()
    for copy in small:
        copy.wait()
    chosen = pick(iota((tenants, count), 0) == tenant_ref[...]).astype(BF16)
    table = jnp.broadcast_to(slot_ref[...].astype(F32), (8, tenants)).astype(BF16)
    slot = dot(table, chosen)[0:1].astype(I32)
    store = slot // per_store
    at_store = pick(iota((stores, count), 0) == store)
    earlier = pick(iota((count, count), 0) < iota((count, count), 1)).astype(BF16)
    before = dot(at_store.astype(BF16), earlier)
    rank = jnp.sum(at_store * before, axis=0, keepdims=True).astype(I32)
    placed = iota((places, count), 0) == store * capacity + rank
    hot = pick(placed).astype(BF16)
    place_ref[...] = hot
    for n in range(chunks):
        load(n).wait()
        span = slice(n * step, (n + 1) * step)
        out[:, span] = dot(hot, rows[:, span]).astype(BF16)
    number = iota((1, count), 1) + 1
    lane_of = iota((LANES, count), 0) % (LANES // 2)
    spread = jnp.where(lane_of == group * capacity + rank, number, 0).astype(F32).astype(BF16)
    by_lane = dot(at_store.astype(BF16), spread, ((1,), (1,)))
    wide = jnp.broadcast_to(by_lane[:, None, :], (stores, capacity, LANES))
    out[:, width : width + LANES] = wide.reshape(places, LANES).astype(BF16)
    slot_col = jnp.sum(jnp.where(placed, slot + 1, 0).astype(F32), axis=1, keepdims=True)
    row_col = jnp.sum(jnp.where(placed, number, 0).astype(F32), axis=1, keepdims=True)
    lane = iota((places, LANES), 1)
    facts = jnp.where(lane == 0, slot_col, jnp.where(lane == 1, row_col, 0.0))
    out[:, width + LANES : width + 2 * LANES] = facts.astype(BF16)


def in_hbm(array):
    return pltpu.with_memory_space_constraint(array, pltpu.HBM)


def pack_rows(row_tenant, tenant_slot, rows, places, per_store):
    count, width = rows.shape
    half = width // CORES
    chunks = 4
    hbm = pl.BlockSpec(memory_space=pltpu.HBM)
    vmem = pl.BlockSpec(memory_space=pltpu.VMEM)
    return pl.pallas_call(
        functools.partial(pack_kernel, per_store),
        out_shape=(
            jax.ShapeDtypeStruct((places, half + 2 * LANES), BF16),
            jax.ShapeDtypeStruct((places, count), BF16),
        ),
        in_specs=[hbm, hbm, hbm],
        out_specs=(vmem, vmem),
        scratch_shapes=[
            pltpu.VMEM((1, count), I32),
            pltpu.VMEM((1, tenant_slot.shape[0]), I32),
            pltpu.VMEM((count, half), BF16),
            pltpu.SemaphoreType.DMA((chunks + 2,)),
        ],
        cost_estimate=COST,
        compiler_params=pltpu.CompilerParams(vmem_limit_bytes=4 << 20),
        name="pack_rows",
    )(
        in_hbm(row_tenant.reshape(1, count)), in_hbm(tenant_slot.reshape(1, -1)), in_hbm(rows)
    )


def route_kernel(group_rows, blocks, mine_ref, expand, facts_ref):
    groups = lax.axis_size("dp")
    places = mine_ref.shape[0]
    width = mine_ref.shape[1] - 2 * LANES
    capacity = places // groups
    block_rows = group_rows * blocks
    by_lane = mine_ref[:, width : width + LANES].astype(F32)
    by_lane = jnp.sum(by_lane.reshape(groups, capacity, LANES), axis=0)[0:1].astype(I32)
    lane = iota((1, LANES), 1)
    home = (lane % places) // capacity * group_rows + by_lane - 1
    home = jnp.where(by_lane > 0, home * blocks + lane // places, -blocks)
    for g in range(groups):
        row = iota((block_rows, LANES), 0) + g * block_rows
        for n, b in enumerate(range(0, blocks, LANES // places)):
            one_hot = pick(row == home + b).astype(BF16)
            expand[g * block_rows : (g + 1) * block_rows, n * LANES : (n + 1) * LANES] = one_hot
    facts_ref[...] = mine_ref[:, width + LANES : width + 2 * LANES].astype(F32)


def routes(mine, groups, group_rows, blocks):
    places = mine.shape[0]
    homes = groups * group_rows * blocks
    vmem = pl.BlockSpec(memory_space=pltpu.VMEM)
    return pl.pallas_call(
        functools.partial(route_kernel, group_rows, blocks),
        out_shape=(
            jax.ShapeDtypeStruct((homes, places * blocks), BF16),
            jax.ShapeDtypeStruct((places, LANES), F32),
        ),
        in_specs=[vmem],
        out_specs=(vmem, vmem),
        compiler_params=pltpu.CompilerParams(vmem_limit_bytes=8 << 20),
        name="routes",
    )(mine)


def query_kernel(
    where_ref, mine_ref, other_ref, facts_ref, tiles_ref, out_ref, *totals
):
    me = lax.axis_index("dp")
    core = lax.axis_index("tensor") % CORES
    slots, per_slot, tile = tiles_ref.shape[:3]
    width = mine_ref.shape[1] - 2 * LANES
    halves = width // tile
    blocks = totals[0].shape[1] // tile
    own_slot = facts_ref[:, 0:1].astype(I32) - 1 - me * slots
    for total in totals:
        total[...] = jnp.zeros_like(total)
    for t in range(slots):
        mine = own_slot == t
        for k in range(per_slot):
            place = where_ref[t, k]
            source = lax.shift_right_logical(place, log2(blocks))
            start = lax.shift_left(source & (halves - 1), log2(tile))
            target = lax.shift_left(place & (blocks - 1), log2(tile))
            span = pl.ds(pl.multiple_of(start, tile), tile)
            own_half = lax.shift_right_logical(source, log2(halves)) == core
            rows = jnp.where(own_half, mine_ref[:, span], other_ref[:, span])
            product = dot(rows, tiles_ref[t, k])
            total = totals[k % len(totals)]
            total[:, pl.ds(pl.multiple_of(target, tile), tile)] += jnp.where(mine, product, 0.0)
    whole = totals[0][...]
    for total in totals[1:]:
        whole = whole + total[...]
    sums = [whole[:, b * tile : (b + 1) * tile] for b in range(blocks)]
    out_ref[...] = jnp.concatenate(sums, axis=0).astype(BF16)


def query_visit(mine, other, facts, tiles, where, columns):
    places = mine.shape[0]
    tile = tiles.shape[2]
    vmem = pl.BlockSpec(memory_space=pltpu.VMEM)
    return pl.pallas_call(
        query_kernel,
        out_shape=jax.ShapeDtypeStruct((places * columns // tile, tile), BF16),
        in_specs=[vmem] * 5,
        out_specs=vmem,
        scratch_shapes=[pltpu.VMEM((places, columns), F32)] * 4,
        compiler_params=pltpu.CompilerParams(vmem_limit_bytes=4 << 20),
        name="query_visit",
    )(where, mine, other, facts, tiles)


def send_kernel(expand, stacked_ref, base_ref, out_ref):
    me = lax.axis_index("dp")
    block_rows = base_ref.shape[0]
    for g in range(out_ref.shape[0] // block_rows):
        span = slice(g * block_rows, (g + 1) * block_rows)
        sent = dot(expand[span, :], stacked_ref[...]) + jnp.where(me == g, base_ref[...], 0.0)
        out_ref[span, :] = sent.astype(BF16)


def query_send(expand, stacked, base):
    tile = stacked.shape[1]
    vmem = pl.BlockSpec(memory_space=pltpu.VMEM)
    return pl.pallas_call(
        send_kernel,
        out_shape=jax.ShapeDtypeStruct((expand.shape[0], tile), BF16),
        in_specs=[vmem] * 3,
        out_specs=vmem,
        cost_estimate=COST,
        compiler_params=pltpu.CompilerParams(vmem_limit_bytes=4 << 20),
        name="query_send",
    )(expand, stacked, base.reshape(-1, tile))


def attend_kernel(
    length_ref, arrived_ref, fresh_ref, keys, values, out_ref, raw
):
    requests, kv_heads, context, size = keys.shape
    shards = out_ref.shape[1]
    stores = arrived_ref.shape[0]
    scale = size ** (-0.5)
    query = arrived_ref[0].astype(F32)
    for s in range(1, stores):
        query = query + arrived_ref[s].astype(F32)
    fresh = fresh_ref[...].astype(F32)
    upper = iota((8, size), 0) < 4
    position = iota((1, context), 1)
    mixed = [[None] * kv_heads for _ in range(requests)]
    for i in range(requests):
        heads_of = []
        for g in range(kv_heads):
            first, second = query[2 * g], query[2 * g + 1]
            if i == 0:
                heads = jnp.where(upper, first, pltpu.roll(second, 4, 0))
            else:
                heads = jnp.where(upper, pltpu.roll(first, 4, 0), second)
            heads_of.append(heads.astype(BF16))
            raw[g] = dot(heads_of[g], keys[i, g], ((1,), (1,))) * scale
        visible = position < length_ref[0, i]
        parts = []
        for g in range(kv_heads):
            heads, scores = heads_of[g], raw[g]
            fresh_key = fresh[i, 0:1, g * size : (g + 1) * size]
            own = jnp.sum(heads.astype(F32) * fresh_key, axis=1, keepdims=True) * scale
            scores = jnp.where(visible, scores, -1e30)
            highest = jnp.maximum(jnp.max(scores, axis=1, keepdims=True), own)
            weights = jnp.where(visible, jnp.exp(scores - highest), 0.0)
            own_weight = jnp.exp(own - highest)
            total = jnp.sum(weights, axis=1, keepdims=True) + own_weight
            share = (weights / total).astype(BF16)
            own_share = (own_weight / total).astype(BF16).astype(F32)
            parts.append((share, own_share))
        for g in range(kv_heads):
            share, own_share = parts[g]
            fresh_value = fresh[i, 1:2, g * size : (g + 1) * size]
            mixed[i][g] = dot(share, values[i, g]) + own_share * fresh_value
    for g in range(kv_heads):
        one, two = mixed[0][g], mixed[1][g]
        first = jnp.where(upper, one, pltpu.roll(two, 4, 0)).astype(BF16)
        second = jnp.where(upper, pltpu.roll(one, 4, 0), two).astype(BF16)
        for d in range(out_ref.shape[0]):
            out_ref[d, 2 * g] = first
            out_ref[d, 2 * g + 1] = second


def attend(arrived, keys, values, fresh, lengths, groups):
    requests, kv_heads, context, size = keys.shape
    shards = arrived.shape[0] // (groups * 8)
    vmem = pl.BlockSpec(memory_space=pltpu.VMEM)
    return pl.pallas_call(
        attend_kernel,
        out_shape=jax.ShapeDtypeStruct((groups, shards, 8, size), BF16),
        in_specs=[vmem] * 5,
        scratch_shapes=[
            pltpu.VMEM((kv_heads, 8, context), F32),
        ],
        compiler_params=pltpu.CompilerParams(vmem_limit_bytes=4 << 20),
        name="attend",
    )(lengths.reshape(1, -1), arrived.reshape(groups, shards, 8, size), fresh, keys, values)


def output_kernel(
    where_ref, arrived_ref, facts_ref, tiles_ref, weight, out_ref, rows_ref, total_ref, hold
):
    me = lax.axis_index("dp")
    other = 1 - lax.axis_index("tensor") % CORES
    slots, per_slot, tile = tiles_ref.shape[:3]
    groups, shards, capacity, columns = out_ref.shape
    places = groups * capacity
    depth, width = weight.shape
    blocks = depth // tile
    group_rows = arrived_ref.shape[0] // (groups * blocks)
    facts = facts_ref[...].astype(I32)
    own_slot = facts[:, 0:1] - 1 - me * slots
    number = facts[:, 1:2]
    home = iota((places, 1), 0) // capacity * group_rows + number - 1
    home = jnp.where(number > 0, home * blocks, -blocks)
    total_ref[...] = jnp.zeros_like(total_ref)
    lane = iota((places, arrived_ref.shape[0]), 1)
    gather = jnp.concatenate([pick(lane == home + b).astype(BF16) for b in range(blocks)], axis=0)
    gathered = dot(gather, arrived_ref[...]).astype(BF16)
    for b in range(blocks):
        rows_ref[:, b * tile : (b + 1) * tile] = gathered[b * places : (b + 1) * places]
    targets = width // tile
    every = slots * per_slot // shards
    for shard in range(shards):
        for n in range(shard * every, (shard + 1) * every):
            t, k = n // per_slot, n % per_slot
            place = where_ref[t, k]
            source = lax.shift_left(lax.shift_right_logical(place, log2(targets)), log2(tile))
            target = lax.shift_left(place & (targets - 1), log2(tile))
            rows = rows_ref[:, pl.ds(pl.multiple_of(source, tile), tile)]
            product = dot(rows, tiles_ref[t, k])
            span = pl.ds(pl.multiple_of(target, tile), tile)
            total_ref[:, span] += jnp.where(own_slot == t, product, 0.0)
        hold[shard] = dot(rows_ref[...], weight[:, columns_of(shard, other, columns)])
    for shard in range(shards):
        result = hold[shard] + total_ref[:, columns_of(shard, other, columns)]
        out_ref[:, shard] = result.reshape(groups, capacity, columns).astype(BF16)


def columns_of(shard, half, columns):
    return pl.ds(pl.multiple_of((shard * CORES + half) * columns, columns), columns)


def output_visit(arrived, facts, tiles, where, weight, groups):
    depth, width = weight.shape
    places = facts.shape[0]
    shards = width // depth
    vmem = pl.BlockSpec(memory_space=pltpu.VMEM)
    return pl.pallas_call(
        output_kernel,
        out_shape=(
            jax.ShapeDtypeStruct((groups, shards, places // groups, depth // CORES), BF16),
            jax.ShapeDtypeStruct((places, depth), BF16),
            jax.ShapeDtypeStruct((places, width), F32),
        ),
        in_specs=[vmem] * 5,
        out_specs=(vmem, vmem, vmem),
        scratch_shapes=[pltpu.VMEM((shards, places, depth // CORES), F32)],
        cost_estimate=COST,
        compiler_params=pltpu.CompilerParams(vmem_limit_bytes=16 << 20),
        name="output_visit",
    )(where, arrived, facts, tiles, weight)


def own_kernel(rows_ref, weight, total_ref, out_ref):
    core = lax.axis_index("tensor") % CORES
    groups, shards, capacity, columns = out_ref.shape
    for shard in range(shards):
        span = columns_of(shard, core, columns)
        result = dot(rows_ref[...], weight[:, span]) + total_ref[:, span]
        out_ref[:, shard] = result.reshape(groups, capacity, columns)


def output_own(rows, weight, total, shape):
    vmem = pl.BlockSpec(memory_space=pltpu.VMEM)
    return pl.pallas_call(
        own_kernel,
        out_shape=jax.ShapeDtypeStruct(shape, F32),
        in_specs=[vmem, vmem, vmem],
        out_specs=vmem,
        cost_estimate=COST,
        compiler_params=pltpu.CompilerParams(vmem_limit_bytes=16 << 20),
        name="output_own",
    )(rows, weight, total)


def finish_kernel(arrived_ref, place_ref, out_ref):
    stores, pairs, cores, capacity, columns = arrived_ref.shape
    for core in range(cores):
        total = arrived_ref[:, 0, core].astype(F32)
        for pair in range(1, pairs):
            total = total + arrived_ref[:, pair, core].astype(F32)
        rounded = total.reshape(stores * capacity, columns).astype(BF16)
        span = slice(core * columns, (core + 1) * columns)
        out_ref[:, span] = dot(place_ref[...], rounded, ((0,), (0,))).astype(BF16)


def finish(arrived, place):
    cores, columns = arrived.shape[2], arrived.shape[4]
    return pl.pallas_call(
        finish_kernel,
        out_shape=jax.ShapeDtypeStruct((place.shape[1], cores * columns), BF16),
        compiler_params=pltpu.CompilerParams(vmem_limit_bytes=8 << 20),
        name="finish",
    )(arrived, place)


def across_chip(block):
    count = lax.axis_size("tensor")
    return lax.ppermute(block, "tensor", [(i, i ^ 1) for i in range(count)])


def swap(blocks, axes):
    return lax.all_to_all(blocks, axes, split_axis=0, concat_axis=0, tiled=True)


def body(
    activations,
    query_weight,
    output_weight,
    key_cache,
    value_cache,
    fresh_pair,
    cache_length,
    row_tenant,
    tenant_slot,
    query_deltas,
    query_where,
    output_deltas,
    output_where,
):
    groups = lax.axis_size("dp")
    shards = lax.axis_size("tensor")
    per_store = query_deltas.shape[0]
    capacity = 8
    packed, place = pack_rows(row_tenant, tenant_slot, activations, groups * capacity, per_store)
    arrived = swap(packed.reshape(groups, capacity, -1), "dp").reshape(packed.shape)
    base_query = jnp.dot(activations, query_weight, preferred_element_type=F32)
    other = across_chip(arrived)
    blocks = base_query.shape[1] // LANES
    expand, facts = routes(arrived, groups, activations.shape[0], blocks)
    products = query_visit(
        arrived, other, facts, query_deltas, query_where, base_query.shape[1]
    )
    sent_query = query_send(expand, products, base_query)
    query = swap(sent_query, EVERY)
    attended = attend(query, key_cache, value_cache, fresh_pair, cache_length, groups)
    size = attended.shape[3]
    rows = swap(attended.reshape(-1, size), EVERY)
    sent, visitors, delta = output_visit(
        rows, facts, output_deltas, output_where, output_weight, groups
    )
    received = across_chip(sent)
    own = output_own(visitors, output_weight, delta, sent.shape)
    parts = (own + received.astype(F32)).astype(BF16)
    columns = parts.shape[3]
    summed = swap(parts.reshape(-1, columns), EVERY)
    return finish(summed.reshape(groups, shards // CORES, CORES, capacity, columns), place)


def solution(mesh):
    placed = (
        P("dp", None),
        P(None, "tensor"),
        P("tensor", None),
        P(("dp", "tensor"), None, None, None),
        P(("dp", "tensor"), None, None, None),
        P(("dp", "tensor"), None, None),
        P(("dp", "tensor")),
        P("dp"),
        P(),
        P("dp", "tensor", None, None),
        P("dp", "tensor"),
        P("dp", "tensor", None, None),
        P("dp", "tensor"),
    )
    return jax.shard_map(
        body, mesh=mesh, in_specs=placed, out_specs=P("dp", "tensor"), check_vma=False
    )
```

```python
import functools

import jax
import jax.numpy as jnp
from jax import lax
from jax.experimental import pallas as pl
from jax.experimental.pallas import tpu as pltpu
from jax.sharding import PartitionSpec as P

F32 = jnp.float32
BF16 = jnp.bfloat16
I32 = jnp.int32
LANES = 128
CORES = 2
EVERY = ("dp", "tensor")
COST = pl.CostEstimate(flops=1 << 35, bytes_accessed=48 << 20, transcendentals=0)


def iota(shape, axis):
    return lax.broadcasted_iota(I32, shape, axis)


def dot(a, b, contract=((1,), (0,))):
    return lax.dot_general(a, b, (contract, ((), ())), preferred_element_type=F32)


def log2(size):
    return size.bit_length() - 1


def pick(mask, value=1.0):
    return jnp.where(mask, value, 0.0)


def pack_kernel(
    per_store, tenant_hbm, slot_hbm, rows_hbm, out, place_ref, tenant_ref, slot_ref, rows, sems
):
    group = lax.axis_index("dp")
    core = lax.axis_index("tensor") % CORES
    count, width = rows.shape
    tenants = slot_ref.shape[1]
    places = out.shape[0]
    capacity = 8
    stores = places // capacity
    chunks = sems.shape[0] - 2
    step = width // chunks

    def load(n):
        source = pl.ds(pl.multiple_of(core * width + n * step, LANES), step)
        target = pl.ds(n * step, step)
        return pltpu.make_async_copy(rows_hbm.at[:, source], rows.at[:, target], sems.at[n])

    small = (
        pltpu.make_async_copy(tenant_hbm, tenant_ref, sems.at[chunks]),
        pltpu.make_async_copy(slot_hbm, slot_ref, sems.at[chunks + 1]),
    )
    for copy in small:
        copy.start()
    for n in range(chunks):
        load(n).start()
    for copy in small:
        copy.wait()
    chosen = pick(iota((tenants, count), 0) == tenant_ref[...]).astype(BF16)
    table = jnp.broadcast_to(slot_ref[...].astype(F32), (8, tenants)).astype(BF16)
    slot = dot(table, chosen)[0:1].astype(I32)
    store = slot // per_store
    at_store = pick(iota((stores, count), 0) == store)
    earlier = pick(iota((count, count), 0) < iota((count, count), 1)).astype(BF16)
    before = dot(at_store.astype(BF16), earlier)
    rank = jnp.sum(at_store * before, axis=0, keepdims=True).astype(I32)
    placed = iota((places, count), 0) == store * capacity + rank
    hot = pick(placed).astype(BF16)
    place_ref[...] = hot
    for n in range(chunks):
        load(n).wait()
        span = slice(n * step, (n + 1) * step)
        out[:, span] = dot(hot, rows[:, span]).astype(BF16)
    number = iota((1, count), 1) + 1
    lane_of = iota((LANES, count), 0) % (LANES // 2)
    spread = jnp.where(lane_of == group * capacity + rank, number, 0).astype(F32).astype(BF16)
    by_lane = dot(at_store.astype(BF16), spread, ((1,), (1,)))
    wide = jnp.broadcast_to(by_lane[:, None, :], (stores, capacity, LANES))
    out[:, width : width + LANES] = wide.reshape(places, LANES).astype(BF16)
    slot_col = jnp.sum(jnp.where(placed, slot + 1, 0).astype(F32), axis=1, keepdims=True)
    row_col = jnp.sum(jnp.where(placed, number, 0).astype(F32), axis=1, keepdims=True)
    lane = iota((places, LANES), 1)
    facts = jnp.where(lane == 0, slot_col, jnp.where(lane == 1, row_col, 0.0))
    out[:, width + LANES : width + 2 * LANES] = facts.astype(BF16)


def in_hbm(array):
    return pltpu.with_memory_space_constraint(array, pltpu.HBM)


def pack_rows(row_tenant, tenant_slot, rows, places, per_store):
    count, width = rows.shape
    half = width // CORES
    chunks = 4
    hbm = pl.BlockSpec(memory_space=pltpu.HBM)
    vmem = pl.BlockSpec(memory_space=pltpu.VMEM)
    return pl.pallas_call(
        functools.partial(pack_kernel, per_store),
        out_shape=(
            jax.ShapeDtypeStruct((places, half + 2 * LANES), BF16),
            jax.ShapeDtypeStruct((places, count), BF16),
        ),
        in_specs=[hbm, hbm, hbm],
        out_specs=(vmem, vmem),
        scratch_shapes=[
            pltpu.VMEM((1, count), I32),
            pltpu.VMEM((1, tenant_slot.shape[0]), I32),
            pltpu.VMEM((count, half), BF16),
            pltpu.SemaphoreType.DMA((chunks + 2,)),
        ],
        cost_estimate=COST,
        compiler_params=pltpu.CompilerParams(vmem_limit_bytes=4 << 20),
        name="pack_rows",
    )(
        in_hbm(row_tenant.reshape(1, count)), in_hbm(tenant_slot.reshape(1, -1)), in_hbm(rows)
    )


def route_kernel(group_rows, blocks, mine_ref, expand, facts_ref):
    groups = lax.axis_size("dp")
    places = mine_ref.shape[0]
    width = mine_ref.shape[1] - 2 * LANES
    capacity = places // groups
    block_rows = group_rows * blocks
    by_lane = mine_ref[:, width : width + LANES].astype(F32)
    by_lane = jnp.sum(by_lane.reshape(groups, capacity, LANES), axis=0)[0:1].astype(I32)
    lane = iota((1, LANES), 1)
    home = (lane % places) // capacity * group_rows + by_lane - 1
    home = jnp.where(by_lane > 0, home * blocks + lane // places, -blocks)
    for g in range(groups):
        row = iota((block_rows, LANES), 0) + g * block_rows
        for n, b in enumerate(range(0, blocks, LANES // places)):
            one_hot = pick(row == home + b).astype(BF16)
            expand[g * block_rows : (g + 1) * block_rows, n * LANES : (n + 1) * LANES] = one_hot
    facts_ref[...] = mine_ref[:, width + LANES : width + 2 * LANES].astype(F32)


def routes(mine, groups, group_rows, blocks):
    places = mine.shape[0]
    homes = groups * group_rows * blocks
    vmem = pl.BlockSpec(memory_space=pltpu.VMEM)
    return pl.pallas_call(
        functools.partial(route_kernel, group_rows, blocks),
        out_shape=(
            jax.ShapeDtypeStruct((homes, places * blocks), BF16),
            jax.ShapeDtypeStruct((places, LANES), F32),
        ),
        in_specs=[vmem],
        out_specs=(vmem, vmem),
        compiler_params=pltpu.CompilerParams(vmem_limit_bytes=8 << 20),
        name="routes",
    )(mine)


def query_kernel(
    where_ref, mine_ref, other_ref, facts_ref, tiles_ref, out_ref, *totals
):
    me = lax.axis_index("dp")
    core = lax.axis_index("tensor") % CORES
    slots, per_slot, tile = tiles_ref.shape[:3]
    width = mine_ref.shape[1] - 2 * LANES
    halves = width // tile
    blocks = totals[0].shape[1] // tile
    own_slot = facts_ref[:, 0:1].astype(I32) - 1 - me * slots
    for total in totals:
        total[...] = jnp.zeros_like(total)
    for t in range(slots):
        mine = own_slot == t
        for k in range(per_slot):
            place = where_ref[t, k]
            source = lax.shift_right_logical(place, log2(blocks))
            start = lax.shift_left(source & (halves - 1), log2(tile))
            target = lax.shift_left(place & (blocks - 1), log2(tile))
            span = pl.ds(pl.multiple_of(start, tile), tile)
            own_half = lax.shift_right_logical(source, log2(halves)) == core
            rows = jnp.where(own_half, mine_ref[:, span], other_ref[:, span])
            product = dot(rows, tiles_ref[t, k])
            total = totals[k % len(totals)]
            total[:, pl.ds(pl.multiple_of(target, tile), tile)] += jnp.where(mine, product, 0.0)
    whole = totals[0][...]
    for total in totals[1:]:
        whole = whole + total[...]
    sums = [whole[:, b * tile : (b + 1) * tile] for b in range(blocks)]
    out_ref[...] = jnp.concatenate(sums, axis=0).astype(BF16)


def query_visit(mine, other, facts, tiles, where, columns):
    places = mine.shape[0]
    tile = tiles.shape[2]
    vmem = pl.BlockSpec(memory_space=pltpu.VMEM)
    return pl.pallas_call(
        query_kernel,
        out_shape=jax.ShapeDtypeStruct((places * columns // tile, tile), BF16),
        in_specs=[vmem] * 5,
        out_specs=vmem,
        scratch_shapes=[pltpu.VMEM((places, columns), F32)] * 4,
        compiler_params=pltpu.CompilerParams(vmem_limit_bytes=4 << 20),
        name="query_visit",
    )(where, mine, other, facts, tiles)


def send_kernel(expand, stacked_ref, base_ref, out_ref):
    me = lax.axis_index("dp")
    block_rows = base_ref.shape[0]
    for g in range(out_ref.shape[0] // block_rows):
        span = slice(g * block_rows, (g + 1) * block_rows)
        sent = dot(expand[span, :], stacked_ref[...]) + jnp.where(me == g, base_ref[...], 0.0)
        out_ref[span, :] = sent.astype(BF16)


def query_send(expand, stacked, base):
    tile = stacked.shape[1]
    vmem = pl.BlockSpec(memory_space=pltpu.VMEM)
    return pl.pallas_call(
        send_kernel,
        out_shape=jax.ShapeDtypeStruct((expand.shape[0], tile), BF16),
        in_specs=[vmem] * 3,
        out_specs=vmem,
        cost_estimate=COST,
        compiler_params=pltpu.CompilerParams(vmem_limit_bytes=4 << 20),
        name="query_send",
    )(expand, stacked, base.reshape(-1, tile))


def attend_kernel(
    length_ref, arrived_ref, fresh_ref, keys, values, out_ref, raw
):
    requests, kv_heads, context, size = keys.shape
    shards = out_ref.shape[1]
    stores = arrived_ref.shape[0]
    scale = size ** (-0.5)
    query = arrived_ref[0].astype(F32)
    for s in range(1, stores):
        query = query + arrived_ref[s].astype(F32)
    fresh = fresh_ref[...].astype(F32)
    upper = iota((8, size), 0) < 4
    position = iota((1, context), 1)
    mixed = [[None] * kv_heads for _ in range(requests)]
    heads_of = {}

    def score(i, g):
        first, second = query[2 * g], query[2 * g + 1]
        if i == 0:
            heads = jnp.where(upper, first, pltpu.roll(second, 4, 0))
        else:
            heads = jnp.where(upper, pltpu.roll(first, 4, 0), second)
        heads_of[i, g] = heads.astype(BF16)
        raw[i, g] = dot(heads_of[i, g], keys[i, g], ((1,), (1,))) * scale

    def soften(i, g):
        visible = position < length_ref[0, i]
        heads, scores = heads_of[i, g], raw[i, g]
        fresh_key = fresh[i, 0:1, g * size : (g + 1) * size]
        own = jnp.sum(heads.astype(F32) * fresh_key, axis=1, keepdims=True) * scale
        scores = jnp.where(visible, scores, -1e30)
        highest = jnp.maximum(jnp.max(scores, axis=1, keepdims=True), own)
        weights = jnp.where(visible, jnp.exp(scores - highest), 0.0)
        own_weight = jnp.exp(own - highest)
        inverse = 1.0 / (jnp.sum(weights, axis=1, keepdims=True) + own_weight)
        share = (weights * inverse).astype(BF16)
        own_share = (own_weight * inverse).astype(BF16).astype(F32)
        fresh_value = fresh[i, 1:2, g * size : (g + 1) * size]
        mixed[i][g] = dot(share, values[i, g]) + own_share * fresh_value

    units = [(i, g) for i in range(requests) for g in range(kv_heads)]
    ahead = 3
    for n in range(len(units) + ahead):
        if n < len(units):
            score(*units[n])
        if n >= ahead:
            soften(*units[n - ahead])
    for g in range(kv_heads):
        one, two = mixed[0][g], mixed[1][g]
        first = jnp.where(upper, one, pltpu.roll(two, 4, 0)).astype(BF16)
        second = jnp.where(upper, pltpu.roll(one, 4, 0), two).astype(BF16)
        for d in range(out_ref.shape[0]):
            out_ref[d, 2 * g] = first
            out_ref[d, 2 * g + 1] = second


def attend(arrived, keys, values, fresh, lengths, groups):
    requests, kv_heads, context, size = keys.shape
    shards = arrived.shape[0] // (groups * 8)
    vmem = pl.BlockSpec(memory_space=pltpu.VMEM)
    return pl.pallas_call(
        attend_kernel,
        out_shape=jax.ShapeDtypeStruct((groups, shards, 8, size), BF16),
        in_specs=[vmem] * 5,
        scratch_shapes=[
            pltpu.VMEM((requests, kv_heads, 8, context), F32),
        ],
        compiler_params=pltpu.CompilerParams(vmem_limit_bytes=4 << 20),
        name="attend",
    )(lengths.reshape(1, -1), arrived.reshape(groups, shards, 8, size), fresh, keys, values)


def output_kernel(
    where_ref, arrived_ref, facts_ref, tiles_ref, weight, out_ref, rows_ref, total_ref, hold
):
    me = lax.axis_index("dp")
    other = 1 - lax.axis_index("tensor") % CORES
    slots, per_slot, tile = tiles_ref.shape[:3]
    groups, shards, capacity, columns = out_ref.shape
    places = groups * capacity
    depth, width = weight.shape
    blocks = depth // tile
    own_slot = facts_ref[:, 0:1].astype(I32) - 1 - me * slots
    total_ref[...] = jnp.zeros_like(total_ref)
    span = arrived_ref.shape[0] // groups
    lane = iota((capacity, span), 1)
    taken = []
    for g in range(groups):
        number = facts_ref[g * capacity : (g + 1) * capacity, 1:2].astype(I32)
        home = jnp.where(number > 0, (number - 1) * blocks, -blocks)
        take = jnp.concatenate([pick(lane == home + b) for b in range(blocks)], axis=0)
        taken.append(dot(take.astype(BF16), arrived_ref[g * span : (g + 1) * span, :]))
    for b in range(blocks):
        block = [piece[b * capacity : (b + 1) * capacity] for piece in taken]
        rows_ref[:, b * tile : (b + 1) * tile] = jnp.concatenate(block, axis=0).astype(BF16)
    targets = width // tile
    every = slots * per_slot // shards
    for shard in range(shards):
        for n in range(shard * every, (shard + 1) * every):
            t, k = n // per_slot, n % per_slot
            place = where_ref[t, k]
            source = lax.shift_left(lax.shift_right_logical(place, log2(targets)), log2(tile))
            target = lax.shift_left(place & (targets - 1), log2(tile))
            rows = rows_ref[:, pl.ds(pl.multiple_of(source, tile), tile)]
            product = dot(rows, tiles_ref[t, k])
            span = pl.ds(pl.multiple_of(target, tile), tile)
            total_ref[:, span] += jnp.where(own_slot == t, product, 0.0)
        hold[shard] = dot(rows_ref[...], weight[:, columns_of(shard, other, columns)])
    for shard in range(shards):
        result = hold[shard] + total_ref[:, columns_of(shard, other, columns)]
        out_ref[:, shard] = result.reshape(groups, capacity, columns).astype(BF16)


def columns_of(shard, half, columns):
    return pl.ds(pl.multiple_of((shard * CORES + half) * columns, columns), columns)


def output_visit(arrived, facts, tiles, where, weight, groups):
    depth, width = weight.shape
    places = facts.shape[0]
    shards = width // depth
    vmem = pl.BlockSpec(memory_space=pltpu.VMEM)
    return pl.pallas_call(
        output_kernel,
        out_shape=(
            jax.ShapeDtypeStruct((groups, shards, places // groups, depth // CORES), BF16),
            jax.ShapeDtypeStruct((places, depth), BF16),
            jax.ShapeDtypeStruct((places, width), F32),
        ),
        in_specs=[vmem] * 5,
        out_specs=(vmem, vmem, vmem),
        scratch_shapes=[pltpu.VMEM((shards, places, depth // CORES), F32)],
        cost_estimate=COST,
        compiler_params=pltpu.CompilerParams(vmem_limit_bytes=16 << 20),
        name="output_visit",
    )(where, arrived, facts, tiles, weight)


def own_kernel(rows_ref, weight, total_ref, out_ref):
    core = lax.axis_index("tensor") % CORES
    groups, shards, capacity, columns = out_ref.shape
    for shard in range(shards):
        span = columns_of(shard, core, columns)
        result = dot(rows_ref[...], weight[:, span]) + total_ref[:, span]
        out_ref[:, shard] = result.reshape(groups, capacity, columns)


def output_own(rows, weight, total, shape):
    vmem = pl.BlockSpec(memory_space=pltpu.VMEM)
    return pl.pallas_call(
        own_kernel,
        out_shape=jax.ShapeDtypeStruct(shape, F32),
        in_specs=[vmem, vmem, vmem],
        out_specs=vmem,
        cost_estimate=COST,
        compiler_params=pltpu.CompilerParams(vmem_limit_bytes=16 << 20),
        name="output_own",
    )(rows, weight, total)


def finish_kernel(arrived_ref, place_ref, out_ref):
    stores, pairs, cores, capacity, columns = arrived_ref.shape
    for core in range(cores):
        total = arrived_ref[:, 0, core].astype(F32)
        for pair in range(1, pairs):
            total = total + arrived_ref[:, pair, core].astype(F32)
        rounded = total.reshape(stores * capacity, columns).astype(BF16)
        span = slice(core * columns, (core + 1) * columns)
        out_ref[:, span] = dot(place_ref[...], rounded, ((0,), (0,))).astype(BF16)


def finish(arrived, place):
    cores, columns = arrived.shape[2], arrived.shape[4]
    return pl.pallas_call(
        finish_kernel,
        out_shape=jax.ShapeDtypeStruct((place.shape[1], cores * columns), BF16),
        compiler_params=pltpu.CompilerParams(vmem_limit_bytes=8 << 20),
        name="finish",
    )(arrived, place)


def across_chip(block):
    count = lax.axis_size("tensor")
    return lax.ppermute(block, "tensor", [(i, i ^ 1) for i in range(count)])


def swap(blocks, axes):
    return lax.all_to_all(blocks, axes, split_axis=0, concat_axis=0, tiled=True)


def body(
    activations,
    query_weight,
    output_weight,
    key_cache,
    value_cache,
    fresh_pair,
    cache_length,
    row_tenant,
    tenant_slot,
    query_deltas,
    query_where,
    output_deltas,
    output_where,
):
    groups = lax.axis_size("dp")
    shards = lax.axis_size("tensor")
    per_store = query_deltas.shape[0]
    capacity = 8
    packed, place = pack_rows(row_tenant, tenant_slot, activations, groups * capacity, per_store)
    arrived = swap(packed.reshape(groups, capacity, -1), "dp").reshape(packed.shape)
    base_query = jnp.dot(activations, query_weight, preferred_element_type=F32)
    other = across_chip(arrived)
    blocks = base_query.shape[1] // LANES
    expand, facts = routes(arrived, groups, activations.shape[0], blocks)
    products = query_visit(
        arrived, other, facts, query_deltas, query_where, base_query.shape[1]
    )
    sent_query = query_send(expand, products, base_query)
    query = swap(sent_query, EVERY)
    attended = attend(query, key_cache, value_cache, fresh_pair, cache_length, groups)
    size = attended.shape[3]
    rows = swap(attended.reshape(-1, size), EVERY)
    sent, visitors, delta = output_visit(
        rows, facts, output_deltas, output_where, output_weight, groups
    )
    received = across_chip(sent)
    own = output_own(visitors, output_weight, delta, sent.shape)
    parts = (own + received.astype(F32)).astype(BF16)
    columns = parts.shape[3]
    summed = swap(parts.reshape(-1, columns), EVERY)
    return finish(summed.reshape(groups, shards // CORES, CORES, capacity, columns), place)


def solution(mesh):
    placed = (
        P("dp", None),
        P(None, "tensor"),
        P("tensor", None),
        P(("dp", "tensor"), None, None, None),
        P(("dp", "tensor"), None, None, None),
        P(("dp", "tensor"), None, None),
        P(("dp", "tensor")),
        P("dp"),
        P(),
        P("dp", "tensor", None, None),
        P("dp", "tensor"),
        P("dp", "tensor", None, None),
        P("dp", "tensor"),
    )
    return jax.shard_map(
        body, mesh=mesh, in_specs=placed, out_specs=P("dp", "tensor"), check_vma=False
    )
```
